32 devices in a mesh: gx: 2 (over x), gy: 4 (over z), lev: 4 (over y, core).
Axes of the slice: x: 2, y: 2, z: 4, core: 2. Of those that a mesh axis runs over, the one named last changes fastest.
Arguments:
- zonal: float32 [128, 64, 512], P('lev', 'gx', 'gy'), may hold values from -6 to 6
- meridional: float32 [128, 64, 512], P('lev', 'gx', 'gy'), may hold values from -6 to 6
- vertical: float32 [128, 64, 512], P('lev', 'gx', 'gy'), may hold values from -4 to 4
- pressure: float32 [128, 64, 512], P('lev', 'gx', 'gy'), may hold values from -6 to 6
- coupling: float32 [128, 64, 512], P('lev', 'gx', 'gy'), may hold values from 0.125 to 32768
- surface: int32 [64, 512], P('gx', 'gy'), may hold values from 0 to 16
- lid_flag: int32 [64, 512], P('gx', 'gy'), may hold values from 0 to 1
Outputs:
- zonal_out: float32 [128, 64, 512], P('lev', 'gx', 'gy')
- meridional_out: float32 [128, 64, 512], P('lev', 'gx', 'gy')
- vertical_out: float32 [128, 64, 512], P('lev', 'gx', 'gy')
- pressure_out: float32 [128, 64, 512], P('lev', 'gx', 'gy')
The draws below stay inside these ranges and needn't reach their ends.
Inputs may be any that keep to these rules, and one draw needn't show every extreme that they name: `surface`: the number of lowest levels of a column that lie below the terrain. `lid_flag`: 1 closes the column's top with a rigid lid, 0 leaves it open.
All inputs are finite; a program needn't handle non-finite values.
Results may differ from the reference program's by a relative error of at most 0.0003.
Values sent between devices are 32-bit elements; how exact they have to be, the bound alone decides.
No kernel may reach another device: no remote copies, remote signals or barrier semaphores. Data moves between devices by JAX's collectives and lax.ppermute only.
A program may use at most 128 MiB of HBM per device.

```python
import math
import jax
import jax.numpy as jnp
from jax import lax

LZ = 32
SUBSTEPS = 3
NZ = 128
NX = 64
NY = 512


def draw_vertical(key, part):
    values = jnp.clip(jax.random.normal(key, (NZ, NX, NY), jnp.float32), -4.0, 4.0)
    return values


def draw_coupling(key, part):
    column_key = jax.random.fold_in(key, 11)
    level_key = jax.random.fold_in(key, 23)
    column_high = math.log(16.0 * LZ * LZ)
    column_log = jax.random.uniform(column_key, (NX, NY), jnp.float32, math.log(0.25), column_high)
    column_scale = jnp.exp(column_log)
    rough_log = jax.random.uniform(level_key, (NZ, NX, NY), jnp.float32, math.log(0.5), math.log(2.0))
    rough = jnp.exp(rough_log)
    return column_scale[None] * rough


def touch_ends(drawn, stream_key, low, top_value):
    longest = drawn.shape.index(max(drawn.shape))
    spots = []
    for shift in (0, 1):
        where = [jax.random.randint(jax.random.fold_in(stream_key, axis), (), 0, length) for axis, length in enumerate(drawn.shape)]
        where[longest] = (where[longest] + shift) % drawn.shape[longest]
        spots.append(tuple(where))
    return drawn.at[spots[0]].set(low).at[spots[1]].set(top_value)


def level_of(own_key, dims, pieces, smallest, top_value):
    level, own = 1.0, jax.random.fold_in(own_key, 6)
    for dim, blocks in pieces:
        draws = jnp.exp(jax.random.uniform(jax.random.fold_in(own, dim), (blocks,), jnp.float32, smallest / len(pieces), top_value / len(pieces)))
        level = level * jnp.repeat(draws, dims[dim] // blocks).reshape([-1 if axis == dim else 1 for axis in range(len(dims))])
    return level


def centred(key, shape, scale, reach, cuts=(), dtype=jnp.bfloat16):
    result = scale * jax.random.normal(key, shape, jnp.float32)
    if cuts:
        result = result * level_of(key, shape, cuts, -0.22, 0.18)
    return jnp.clip(result, -reach, reach).astype(dtype)


def setup_inputs(seed: int = 0) -> dict:
    splits = jax.random.split(jax.random.key(seed), 8)
    return {
        "zonal": centred(splits[0], (NZ, NX, NY), 1.0, 6.0, ((0, 4), (1, 2), (2, 4)), jnp.float32),
        "meridional": centred(splits[1], (NZ, NX, NY), 1.0, 6.0, ((0, 4), (1, 2), (2, 4)), jnp.float32),
        "vertical": draw_vertical(jax.random.fold_in(splits[7], 71), 0),
        "pressure": centred(splits[3], (NZ, NX, NY), 1.0, 6.0, ((0, 4), (1, 2), (2, 4)), jnp.float32),
        "coupling": draw_coupling(jax.random.fold_in(splits[7], 71), 0),
        "surface": touch_ends(jax.random.randint(splits[5], (NX, NY), 0, LZ // 2 + 1), jax.random.fold_in(splits[5], 1), 0, (LZ // 2 + 1) - 1).astype(jnp.int32),
        "lid_flag": touch_ends(jax.random.randint(splits[6], (NX, NY), 0, 2), jax.random.fold_in(splits[6], 1), 0, 1).astype(jnp.int32),
    }


horizontal_step = 0.25
divergence_step = 0.25
vertical_step = 0.5
pressure_step = 0.5


def column_solve(lower, diagonal, upper, source):
    zeros_plane = jnp.zeros(diagonal.shape[1:], jnp.float32)

    def forward(state_pair, level_items):
        ratio_prev, part_prev = state_pair
        low_here, diag_here, up_here, source_here = level_items
        pivots = diag_here - low_here * ratio_prev
        ratio_new = up_here / pivots
        part_new = (source_here - low_here * part_prev) / pivots
        return (ratio_new, part_new), (ratio_new, part_new)

    unused, (ratios, parts) = lax.scan(forward, (zeros_plane, zeros_plane), (lower, diagonal, upper, source))

    def backward(value_next, level_items):
        ratio_here, part_here = level_items
        value = part_here - ratio_here * value_next
        return value, value

    unused_last, solution = lax.scan(backward, zeros_plane, (ratios, parts), reverse=True)
    return solution


def reference(zonal, meridional, vertical, pressure, coupling, surface, lid_flag):
    depth = coupling.shape[0]
    zeros_plane = jnp.zeros((1,) + coupling.shape[1:], jnp.float32)
    coupling_up = jnp.concatenate([coupling[1:], zeros_plane], 0)
    levels = lax.broadcasted_iota(jnp.int32, coupling.shape, 0)
    keep = levels >= surface[None]
    is_top = levels == depth - 1
    lid_value = lid_flag.astype(jnp.float32)[None]
    diagonal = 1.0 + coupling + coupling_up + jnp.where(is_top, lid_value * coupling, 0.0)
    lower = jnp.where(levels == 0, 0.0, -coupling)
    upper = -coupling_up
    diagonal = jnp.where(keep, diagonal, 1.0)
    lower = jnp.where(keep, lower, 0.0)
    upper = jnp.where(keep, upper, 0.0)
    for substep in range(SUBSTEPS):
        zonal = zonal - horizontal_step * (jnp.roll(pressure, -1, 1) - jnp.roll(pressure, 1, 1))
        meridional = meridional - horizontal_step * (jnp.roll(pressure, -1, 2) - jnp.roll(pressure, 1, 2))
        spread = (jnp.roll(zonal, -1, 1) - jnp.roll(zonal, 1, 1)) + (jnp.roll(meridional, -1, 2) - jnp.roll(meridional, 1, 2))
        partial_p = pressure - divergence_step * spread
        above_p = jnp.concatenate([partial_p[1:], zeros_plane], 0)
        below_p = jnp.concatenate([zeros_plane, partial_p[:-1]], 0)
        source = jnp.where(keep, vertical - vertical_step * (above_p - below_p), 0.0)
        vertical = column_solve(lower, diagonal, upper, source)
        previous = jnp.concatenate([zeros_plane, vertical[:-1]], 0)
        pressure = partial_p - pressure_step * (vertical - previous)
    return zonal, meridional, vertical, pressure
```

```python
import functools

import jax
import jax.numpy as jnp
from jax import lax
from jax.experimental import pallas as pl
from jax.experimental.pallas import tpu as pltpu
from jax.sharding import PartitionSpec as P

SUBSTEPS = 3
H_STEP = 0.25
D_STEP = 0.25
V_STEP = 0.5
P_STEP = 0.5
F32 = jnp.float32
PAD = 8

VMEM = pl.BlockSpec(memory_space=pltpu.VMEM)
SMEM = pl.BlockSpec(memory_space=pltpu.SMEM)


def call(kernel, outs, args, scratch=(), smem=0):
    specs = [SMEM] * smem + [VMEM] * (len(args) - smem)
    return pl.pallas_call(
        kernel,
        out_shape=[jax.ShapeDtypeStruct(s, F32) for s in outs],
        in_specs=specs,
        out_specs=[VMEM] * len(outs),
        scratch_shapes=list(scratch),
        compiler_params=pltpu.CompilerParams(vmem_limit_bytes=20 * 1024 * 1024),
    )(*args)


def sides(n):
    return 1 if n <= 2 else 2


def views(refs, rows):
    if len(refs) == 1:
        up = [refs[0].at[r] for r in range(rows)]
        down = [refs[0].at[rows + r] for r in range(rows)]
    else:
        up = [refs[0].at[r] for r in range(rows)]
        down = [refs[1].at[r] for r in range(rows)]
    return up, down


def message_shapes(n, rows, plane):
    if sides(n) == 1:
        return [(2 * rows,) + plane]
    return [(rows,) + plane] * 2


def exchange(messages, axis):
    n = lax.axis_size(axis)
    if n == 1:
        return messages
    up = [(i, (i + 1) % n) for i in range(n)]
    if n == 2:
        return [lax.ppermute(messages[0], axis, up)]
    down = [(j, i) for i, j in up]
    return [lax.ppermute(messages[0], axis, up), lax.ppermute(messages[1], axis, down)]


def source_of(group, m, n):
    return group ^ m if n & (n - 1) == 0 else (group - m) % n


def gather_lev(message):
    n = lax.axis_size("lev")
    got = []
    for m in range(1, n):
        if n & (n - 1) == 0:
            pairs = [(i, i ^ m) for i in range(n)]
        else:
            pairs = [(i, (i + m) % n) for i in range(n)]
        got.append(lax.ppermute(message, "lev", pairs))
    return got


def pack_columns(ref, picks, outs):
    depth, ni, nj = ref.shape
    per = nj // ni
    for b in range(depth // per):
        block = ref[b * per : (b + 1) * per].reshape(per * ni, nj)
        turned = block.T
        for c, out in zip(picks, outs):
            out[b : b + 1, :] = turned[c : c + 1, :]


def send_rows(ref, out_up, out_down, wide):
    ni = ref.shape[1]
    for r in range(wide):
        out_up[r][...] = ref[:, ni - wide + r, :]
        out_down[r][...] = ref[:, r, :]


def first_kernel(sx, sy, zonal, merid, press, *outs):
    mx, my = outs[:sx], outs[sx : sx + sy]
    nj = press.shape[2]
    xu, xd = views(mx, 3)
    send_rows(press, xu[:2], xd[:2], 2)
    send_rows(zonal, xu[2:], xd[2:], 1)
    yu, yd = views(my, 3)
    pack_columns(press, (nj - 2, nj - 1, 0, 1), (yu[0], yu[1], yd[0], yd[1]))
    pack_columns(merid, (nj - 1, 0), (yu[2], yd[2]))


def factor_kernel(groups, group_ref, c, surface, lid, inv, mul, g0, gl, planes):
    depth, ni, nj = c.shape
    last, half = depth - 1, depth // 2
    group = group_ref[0]
    bottom = group == 0
    top = group == groups - 1
    ground = surface[...] - group * depth
    lidf = jnp.where(top, lid[...].astype(F32), 0.0)
    zero = jnp.zeros((ni, nj), F32)

    def coupling(k):
        return jnp.where(ground <= k - 1, c[k], 0.0)

    def diag(k):
        low = c[k] if k > 0 else jnp.where(bottom, c[k], 0.0)
        high = c[k + 1] if k < last else lidf * c[k]
        return 1.0 + low + high

    lo, hi = None, None
    for s in range(half):
        k, j = s, last - s
        d_lo, d_hi = diag(k), diag(j)
        if s:
            e_lo = coupling(k)
            m_lo = e_lo * lo
            mul[k] = m_lo
            d_lo = d_lo - e_lo * m_lo
            e_hi = coupling(j + 1)
            m_hi = e_hi * hi
            mul[j + 1] = m_hi
            d_hi = d_hi - e_hi * m_hi
        if j == half:
            e_mid = coupling(half)
            lo = jnp.where(ground <= k, 1.0 / d_lo, 0.0)
            m_mid = e_mid * lo
            mul[half] = m_mid
            d_hi = d_hi - e_mid * m_mid
        else:
            lo = jnp.where(ground <= k, 1.0 / d_lo, 0.0)
        hi = jnp.where(ground <= j, 1.0 / d_hi, 0.0)
        inv[k] = lo
        inv[j] = hi
    one = jnp.ones((ni, nj), F32)
    t0 = [one] + [None] * (half - 1)
    tl = [one] + [None] * (half - 1)
    for s in range(1, half):
        t0[s] = mul[s] * t0[s - 1]
        tl[s] = mul[last - s + 1] * tl[s - 1]
        g0[s] = t0[s]
        gl[last - s] = tl[s]
    g0[0] = one
    gl[last] = one
    xh0 = inv[half] * (mul[half] * t0[half - 1])
    xhl = inv[half] * tl[half - 1]
    xk0 = inv[half - 1] * t0[half - 1] + mul[half] * xh0
    xkl = mul[half] * xhl
    g0[half], gl[half] = xh0, xhl
    g0[half - 1], gl[half - 1] = xk0, xkl
    for s in range(1, half):
        k, j = half - 1 - s, half + s
        xk0 = inv[k] * g0[k] + mul[k + 1] * xk0
        xkl = mul[k + 1] * xkl
        xh0 = mul[j] * xh0
        xhl = inv[j] * gl[j] + mul[j] * xhl
        g0[k], gl[k] = xk0, xkl
        g0[j], gl[j] = xh0, xhl
    planes[0] = g0[0]
    planes[1] = g0[last]
    planes[2] = gl[last]
    planes[3] = c[0]


def advance_kernel(first, sx, sy, *refs):
    refs = list(refs)
    take = lambda n: [refs.pop(0) for _ in range(n)]
    zonal, merid, vert, press, inv, mul = take(6)
    ox, oy = take(sx), take(sy)
    rx, ry = take(sx), take(sy)
    uh, vh = (None, None) if first else take(2)
    zonal_out, merid_out, y_out, part, planes, uh_out, vh_out = take(7)
    pe, ue, tt, tsq = take(4)
    depth, ni, nj = press.shape
    last, half, per = depth - 1, depth // 2, nj // ni
    wide = 3 if first else 2
    oxu, oxd = views(ox, wide)
    rlo, rhi = views(rx, wide)
    oyu, oyd = views(oy, wide)
    clo, chi = views(ry, wide)

    u_lo = rlo[2][...] if first else uh[0]
    u_hi = rhi[2][...] if first else uh[1]
    u_lo = u_lo - H_STEP * (oxd[0][...] - rlo[0][...])
    u_hi = u_hi - H_STEP * (rhi[1][...] - oxu[1][...])
    uh_out[0], uh_out[1] = u_lo, u_hi
    v_lo = clo[2][...] if first else vh[0]
    v_hi = chi[2][...] if first else vh[1]
    v_lo = v_lo - H_STEP * (oyd[0][...] - clo[0][...])
    v_hi = v_hi - H_STEP * (chi[1][...] - oyu[1][...])
    vh_out[0], vh_out[1] = v_lo, v_hi

    ue[:, PAD - 1, :] = u_lo
    ue[:, PAD + ni, :] = u_hi
    pe[:, PAD - 1, :] = rlo[1][...]
    pe[:, PAD + ni, :] = rhi[0][...]
    p_lo, p_hi = clo[1][...], chi[0][...]
    tsq[...] = jnp.zeros((nj, nj), F32)
    mid = nj // 2
    for b in range(depth // per):
        tsq[0:1, :] = p_hi[b : b + 1]
        tsq[nj - 1 : nj, :] = p_lo[b : b + 1]
        tsq[mid : mid + 1, :] = v_hi[b : b + 1]
        tsq[mid - 1 : mid, :] = v_lo[b : b + 1]
        tt[b * per : (b + 1) * per] = tsq[...].T.reshape(per, ni, nj)

    def copy(k, _):
        pe[k, PAD : PAD + ni, :] = press[k]
        return _

    lax.fori_loop(0, depth, copy, 0, unroll=4)
    lane = lax.broadcasted_iota(jnp.int32, (ni, nj), 1)
    at_first, at_last = lane == 0, lane == nj - 1

    def stencil(k, _):
        p, t = press[k], tt[k]
        u = zonal[k] - H_STEP * (pe[k, PAD + 1 : PAD + 1 + ni, :] - pe[k, PAD - 1 : PAD - 1 + ni, :])
        zonal_out[k] = u
        ue[k, PAD : PAD + ni, :] = u
        right = pltpu.roll(jnp.where(at_first, t, p), nj - 1, 1)
        left = pltpu.roll(jnp.where(at_last, t, p), 1, 1)
        v = merid[k] - H_STEP * (right - left)
        merid_out[k] = v
        t = pltpu.roll(t, mid, 1)
        right = pltpu.roll(jnp.where(at_first, t, v), nj - 1, 1)
        left = pltpu.roll(jnp.where(at_last, t, v), 1, 1)
        spread = (ue[k, PAD + 1 : PAD + 1 + ni, :] - ue[k, PAD - 1 : PAD - 1 + ni, :]) + (right - left)
        part[k] = p - D_STEP * spread
        return _

    lax.fori_loop(0, depth, stencil, 0, unroll=2)

    lo = vert[0] - V_STEP * part[1]
    hi = vert[last] + V_STEP * part[last - 1]
    y_out[0], y_out[last] = lo, hi
    for s in range(1, half):
        k, j = s, last - s
        lo = (vert[k] - V_STEP * (part[k + 1] - part[k - 1])) + mul[k] * lo
        hi = (vert[j] - V_STEP * (part[j + 1] - part[j - 1])) + mul[j + 1] * hi
        y_out[k], y_out[j] = lo, hi
    hi = inv[half] * (hi + mul[half] * lo)
    lo = inv[half - 1] * lo + mul[half] * hi
    y_out[half], y_out[half - 1] = hi, lo
    for s in range(1, half):
        k, j = half - 1 - s, half + s
        lo = inv[k] * y_out[k] + mul[k + 1] * lo
        hi = inv[j] * y_out[j] + mul[j] * hi
        y_out[k], y_out[j] = lo, hi
    planes[0], planes[1] = lo, hi
    planes[2], planes[3] = part[0], part[last]


def finish_kernel(groups, final, sx, sy, group_ref, *refs):
    refs = list(refs)
    take = lambda n: [refs.pop(0) for _ in range(n)]
    y, part, g0, gl = take(4)
    own_s, own_l = take(2)
    got_s, got_l = take(groups - 1), take(groups - 1)
    vert_out, press_out = take(2)
    mx, my = ([], []) if final else (take(sx), take(sy))
    st, lv = take(2)
    depth, ni, nj = y.shape
    group = group_ref[0]
    st[group] = own_s[...]
    lv[group] = own_l[...]
    for m in range(1, groups):
        src = source_of(group, m, groups)
        st[src] = got_s[m - 1][...]
        lv[src] = got_l[m - 1][...]
    zero = jnp.zeros((ni, nj), F32)
    z_top, z_bot = [], []
    for g in range(groups):
        below = V_STEP * lv[g - 1, 3] if g else zero
        above = V_STEP * lv[g + 1, 2] if g < groups - 1 else zero
        z_top.append(lv[g, 0] + st[g, 0] * below - st[g, 1] * above)
        z_bot.append(lv[g, 1] + st[g, 1] * below - st[g, 2] * above)
    ratios, parts = [zero], [zero]
    for g in range(1, groups):
        cg = st[g, 3]
        down = cg * st[g - 1, 1]
        pivot = 1.0 / (1.0 + cg * (st[g - 1, 2] + st[g, 0]) - down * ratios[-1])
        parts.append((cg * (z_bot[g - 1] - z_top[g]) + down * parts[-1]) * pivot)
        ratios.append(cg * st[g, 1] * pivot)
    flux = [zero] * (groups + 1)
    for g in range(groups - 1, 0, -1):
        flux[g] = parts[g] + ratios[g] * flux[g + 1]
    alpha, beta, under = zero, zero, zero
    for g in range(groups):
        mine = group == g
        if g:
            alpha = jnp.where(mine, V_STEP * lv[g - 1, 3] + flux[g], alpha)
            bot = z_bot[g - 1] + st[g - 1, 1] * flux[g - 1] - st[g - 1, 2] * flux[g]
            under = jnp.where(mine, bot, under)
        if g < groups - 1:
            beta = jnp.where(mine, -(V_STEP * lv[g + 1, 2] + flux[g + 1]), beta)

    def level(k, w_prev):
        w = y[k] + g0[k] * alpha + gl[k] * beta
        vert_out[k] = w
        press_out[k] = part[k] - P_STEP * (w - w_prev)
        return w

    lax.fori_loop(0, depth, level, under, unroll=4)
    if not final:
        xu, xd = views(mx, 2)
        send_rows(press_out, xu, xd, 2)
        yu, yd = views(my, 2)
        pack_columns(press_out, (nj - 2, nj - 1, 0, 1), (yu[0], yu[1], yd[0], yd[1]))


def body(zonal, meridional, vertical, pressure, coupling, surface, lid_flag):
    depth, ni, nj = coupling.shape
    full = (depth, ni, nj)
    groups = lax.axis_size("lev")
    group = lax.axis_index("lev").astype(jnp.int32)[None]
    nx, ny = lax.axis_size("gx"), lax.axis_size("gy")
    sx, sy = sides(nx), sides(ny)
    per = nj // ni
    row, col = (depth, nj), (depth // per, nj)

    messages = list(
        call(
            functools.partial(first_kernel, sx, sy),
            message_shapes(nx, 3, row) + message_shapes(ny, 3, col),
            (zonal, meridional, pressure),
        )
    )
    ox, oy = messages[:sx], messages[sx:]
    rx, ry = exchange(ox, "gx"), exchange(oy, "gy")
    inv, mul, g0, gl, own_s = call(
        functools.partial(factor_kernel, groups),
        [full] * 4 + [(4, ni, nj)],
        (group, coupling, surface, lid_flag),
        smem=1,
    )
    got_s = gather_lev(own_s)
    uh = vh = None
    for substep in range(SUBSTEPS):
        first, final = substep == 0, substep == SUBSTEPS - 1
        args = [zonal, meridional, vertical, pressure, inv, mul] + ox + oy + rx + ry
        if not first:
            args += [uh, vh]
        zonal, meridional, y, part, own_l, uh, vh = call(
            functools.partial(advance_kernel, first, sx, sy),
            [full] * 4 + [(4, ni, nj), (2,) + row, (2,) + col],
            args,
            scratch=[
                pltpu.VMEM((depth, ni + 2 * PAD, nj), F32),
                pltpu.VMEM((depth, ni + 2 * PAD, nj), F32),
                pltpu.VMEM(full, F32),
                pltpu.VMEM((nj, nj), F32),
            ],
        )
        got_l = gather_lev(own_l)
        outs = [full, full]
        if not final:
            outs += message_shapes(nx, 2, row) + message_shapes(ny, 2, col)
        results = call(
            functools.partial(finish_kernel, groups, final, sx, sy),
            outs,
            [group, y, part, g0, gl, own_s, own_l] + got_s + got_l,
            scratch=[pltpu.VMEM((groups, 4, ni, nj), F32)] * 2,
            smem=1,
        )
        vertical, pressure = results[:2]
        if not final:
            ox, oy = list(results[2 : 2 + sx]), list(results[2 + sx :])
            rx, ry = exchange(ox, "gx"), exchange(oy, "gy")
    return (zonal, meridional, vertical, pressure)


def solution(mesh):
    block = P("lev", "gx", "gy")
    plane = P("gx", "gy")
    return jax.shard_map(
        body,
        mesh=mesh,
        in_specs=(block,) * 5 + (plane,) * 2,
        out_specs=(block,) * 4,
        check_vma=False,
    )
```

```python
import functools

import jax
import jax.numpy as jnp
from jax import lax
from jax.experimental import pallas as pl
from jax.experimental.pallas import tpu as pltpu
from jax.sharding import PartitionSpec as P

SUBSTEPS = 3
H_STEP = 0.25
D_STEP = 0.25
V_STEP = 0.5
P_STEP = 0.5
F32 = jnp.float32
PAD = 8

VMEM = pl.BlockSpec(memory_space=pltpu.VMEM)
SMEM = pl.BlockSpec(memory_space=pltpu.SMEM)
HBM = pl.BlockSpec(memory_space=pltpu.HBM)


def call(kernel, outs, args, scratch=(), spaces=None, out_spaces=None):
    return list(
        pl.pallas_call(
            kernel,
            out_shape=[jax.ShapeDtypeStruct(s, F32) for s in outs],
            in_specs=spaces or [SMEM] + [VMEM] * (len(args) - 1),
            out_specs=out_spaces or [VMEM] * len(outs),
            scratch_shapes=list(scratch),
            compiler_params=pltpu.CompilerParams(vmem_limit_bytes=20 * 1024 * 1024),
        )(*args)
    )


class Halo:
    def __init__(self, axis, plane):
        self.axis, self.plane = axis, plane
        self.n = lax.axis_size(axis)
        self.count = 1 if self.n <= 2 else 2
        self.swap = self.n > 2 and self.n % 2 == 0

    def shapes(self, rows):
        return [(2 * rows,) + self.plane] if self.count == 1 else [(rows,) + self.plane] * 2

    def scratch(self, rows):
        return pltpu.VMEM((2, rows) + self.plane, F32)

    def write(self, refs, both, even):
        rows = both.shape[1]
        if self.count == 1:
            refs[0][:rows] = both[0]
            refs[0][rows:] = both[1]
        elif self.swap:
            refs[0][...] = jnp.where(even, both[0], both[1])
            refs[1][...] = jnp.where(even, both[1], both[0])
        else:
            refs[0][...] = both[0]
            refs[1][...] = both[1]

    def up(self, refs, r, even):
        if self.swap:
            return jnp.where(even, refs[0][r], refs[1][r])
        return refs[0][r]

    def down(self, refs, r, even):
        if self.swap:
            return jnp.where(even, refs[1][r], refs[0][r])
        return refs[0][refs[0].shape[0] // 2 + r] if self.count == 1 else refs[1][r]

    def low(self, refs, r, even):
        if self.swap:
            return jnp.where(even, refs[1][r], refs[0][r])
        return refs[0][r]

    def high(self, refs, r, even):
        if self.swap:
            return jnp.where(even, refs[0][r], refs[1][r])
        return refs[0][refs[0].shape[0] // 2 + r] if self.count == 1 else refs[1][r]

    def exchange(self, messages):
        n = self.n
        if n == 1:
            return messages
        if self.swap:
            first = [(i, i ^ 1) for i in range(n)]
            second = [(i, (i + 1) % n if i % 2 else (i - 1) % n) for i in range(n)]
            got = lax.ppermute(messages[1], self.axis, second)
            return [lax.ppermute(messages[0], self.axis, first), got]
        up = [(i, (i + 1) % n) for i in range(n)]
        if n == 2:
            return [lax.ppermute(messages[0], self.axis, up)]
        down = [(j, i) for i, j in up]
        return [lax.ppermute(messages[0], self.axis, up), lax.ppermute(messages[1], self.axis, down)]


def to_lev(message, m):
    n = lax.axis_size("lev")
    if n & (n - 1) == 0:
        return lax.ppermute(message, "lev", [(i, i ^ m) for i in range(n)])
    return lax.ppermute(message, "lev", [(i, (i + m) % n) for i in range(n)])


def source_of(group, m, n):
    return group ^ m if n & (n - 1) == 0 else (group - m) % n


def pack_columns(ref, picks, outs):
    depth, ni, nj = ref.shape
    per = nj // ni
    for b in range(depth // per):
        turned = ref[b * per : (b + 1) * per].reshape(per * ni, nj).T
        for c, out in zip(picks, outs):
            out[b : b + 1, :] = turned[c : c + 1, :]


def pack_pressure(press, both_x, both_y):
    ni, nj = press.shape[1:]
    for r in range(2):
        both_x[0, r] = press[:, ni - 2 + r, :]
        both_x[1, r] = press[:, r, :]
    pack_columns(press, (nj - 2, nj - 1, 0, 1), (both_y.at[0, 0], both_y.at[0, 1], both_y.at[1, 0], both_y.at[1, 1]))


def first_kernel(hx, hy, groups, where, *refs):
    zonal, merid, press, coupling, surface, lid = refs[:6]
    u, v, p = refs[6:9]
    mx, my = refs[9 : 9 + hx.count], refs[9 + hx.count : 9 + hx.count + hy.count]
    inv, mul, g0, gl, planes = refs[9 + hx.count + hy.count : 14 + hx.count + hy.count]
    both_x, both_y, c, ground, shut, sems = refs[14 + hx.count + hy.count :]
    pairs = [(press, p), (merid, v), (zonal, u), (coupling, c), (surface, ground), (lid, shut)]
    copies = [pltpu.make_async_copy(a, b, sems.at[n]) for n, (a, b) in enumerate(pairs)]
    for copy in copies:
        copy.start()
    ni, nj = p.shape[1:]
    copies[0].wait()
    pack_pressure(p, both_x, both_y)
    copies[1].wait()
    pack_columns(v, (nj - 1, 0), (both_y.at[0, 2], both_y.at[1, 2]))
    copies[2].wait()
    both_x[0, 2] = u[:, ni - 1, :]
    both_x[1, 2] = u[:, 0, :]
    hx.write(mx, both_x, where[1] == 0)
    hy.write(my, both_y, where[2] == 0)
    for copy in copies[3:]:
        copy.wait()
    factor(groups, where[0], c, ground, shut, inv, mul, g0, gl, planes)


def factor(groups, group, c, surface, lid, inv, mul, g0, gl, planes):
    depth, ni, nj = c.shape
    last, half = depth - 1, depth // 2
    bottom = group == 0
    top = group == groups - 1
    ground = surface[...] - group * depth
    lidf = jnp.where(top, lid[...].astype(F32), 0.0)

    def coupling(k):
        return jnp.where(ground <= k - 1, c[k], 0.0)

    def diag(k):
        low = c[k] if k > 0 else jnp.where(bottom, c[k], 0.0)
        high = c[k + 1] if k < last else lidf * c[k]
        return 1.0 + low + high

    lo, hi = None, None
    for s in range(half):
        k, j = s, last - s
        d_lo, d_hi = diag(k), diag(j)
        if s:
            e_lo = coupling(k)
            m_lo = e_lo * lo
            mul[k] = m_lo
            d_lo = d_lo - e_lo * m_lo
            e_hi = coupling(j + 1)
            m_hi = e_hi * hi
            mul[j + 1] = m_hi
            d_hi = d_hi - e_hi * m_hi
        if j == half:
            e_mid = coupling(half)
            lo = jnp.where(ground <= k, 1.0 / d_lo, 0.0)
            m_mid = e_mid * lo
            mul[half] = m_mid
            d_hi = d_hi - e_mid * m_mid
        else:
            lo = jnp.where(ground <= k, 1.0 / d_lo, 0.0)
        hi = jnp.where(ground <= j, 1.0 / d_hi, 0.0)
        inv[k] = lo
        inv[j] = hi
    one = jnp.ones((ni, nj), F32)
    t0 = [one] + [None] * (half - 1)
    tl = [one] + [None] * (half - 1)
    for s in range(1, half):
        t0[s] = mul[s] * t0[s - 1]
        tl[s] = mul[last - s + 1] * tl[s - 1]
        g0[s] = t0[s]
        gl[last - s] = tl[s]
    g0[0] = one
    gl[last] = one
    xh0 = inv[half] * (mul[half] * t0[half - 1])
    xhl = inv[half] * tl[half - 1]
    xk0 = inv[half - 1] * t0[half - 1] + mul[half] * xh0
    xkl = mul[half] * xhl
    g0[half], gl[half] = xh0, xhl
    g0[half - 1], gl[half - 1] = xk0, xkl
    for s in range(1, half):
        k, j = half - 1 - s, half + s
        xk0 = inv[k] * g0[k] + mul[k + 1] * xk0
        xkl = mul[k + 1] * xkl
        xh0 = mul[j] * xh0
        xhl = inv[j] * gl[j] + mul[j] * xhl
        g0[k], gl[k] = xk0, xkl
        g0[j], gl[j] = xh0, xhl
    planes[0] = g0[0]
    planes[1] = g0[last]
    planes[2] = gl[last]
    planes[3] = c[0]


def condense(group, st, cf):
    half = group // 2
    near = jnp.where(half == 0, 2, 0)
    inner = 1 + half
    outer = 3 * half

    def half_of(inner, outer, near):
        odd = jnp.where(inner == 1, 1, 3)
        c = st[odd, 3]
        x = st[inner, 1]
        kappa = c / (1.0 + c * (st[outer, near] + st[inner, 2 - near]))
        return kappa, st[inner, near] - kappa * x * x, x

    kappa, mine, x = half_of(inner, outer, near)
    _, other, _ = half_of(3 - inner, 3 - outer, 2 - near)
    c = st[2, 3]
    cf[0] = kappa
    cf[1] = mine
    cf[2] = other
    cf[3] = c / (1.0 + c * (mine + other))
    cf[4] = x
    cf[5] = st[outer, near]
    cf[6] = st[inner, 2 - near]


def spread_setup(groups, group, own, got, st):
    st[group] = own[...]
    for m in range(1, groups):
        st[source_of(group, m, groups)] = got[m - 1][...]


def advance_kernel(first, hx, hy, groups, where, *refs):
    refs = list(refs)
    take = lambda n: [refs.pop(0) for _ in range(n)]
    zonal, merid, vert, press, inv, mul = take(6)
    ox, oy = take(hx.count), take(hy.count)
    rx, ry = take(hx.count), take(hy.count)
    paired = groups == 4
    if first:
        own_s = take(1)[0]
        got_s = take(groups - 1)
    else:
        uh, vh = take(2)
        cf = take(1)[0] if paired else None
    zonal_out, merid_out, y_out, part, planes, uh_out, vh_out = take(7)
    across = take(1)[0] if paired else None
    if first:
        st = take(1)[0]
        cf = take(1)[0] if paired else None
    pe, ue, tsq = take(3)
    depth, ni, nj = press.shape
    last, half, per = depth - 1, depth // 2, nj // ni
    group, even_x, even_y = where[0], where[1] == 0, where[2] == 0
    if first:
        spread_setup(groups, group, own_s, got_s, st)
        if paired:
            condense(group, st, cf)

    u_lo = hx.low(rx, 2, even_x) if first else uh[0]
    u_hi = hx.high(rx, 2, even_x) if first else uh[1]
    u_lo = u_lo - H_STEP * (hx.down(ox, 0, even_x) - hx.low(rx, 0, even_x))
    u_hi = u_hi - H_STEP * (hx.high(rx, 1, even_x) - hx.up(ox, 1, even_x))
    uh_out[0], uh_out[1] = u_lo, u_hi
    v_lo = hy.low(ry, 2, even_y) if first else vh[0]
    v_hi = hy.high(ry, 2, even_y) if first else vh[1]
    v_lo = v_lo - H_STEP * (hy.down(oy, 0, even_y) - hy.low(ry, 0, even_y))
    v_hi = v_hi - H_STEP * (hy.high(ry, 1, even_y) - hy.up(oy, 1, even_y))
    vh_out[0], vh_out[1] = v_lo, v_hi

    ue[:, PAD - 1, :] = u_lo
    ue[:, PAD + ni, :] = u_hi
    pe[:, PAD - 1, :] = hx.low(rx, 1, even_x)
    pe[:, PAD + ni, :] = hx.high(rx, 0, even_x)
    p_lo, p_hi = hy.low(ry, 1, even_y), hy.high(ry, 0, even_y)
    rows = per * ni
    src = lax.broadcasted_iota(jnp.int32, (2 * nj, nj), 0) % nj
    dst = lax.broadcasted_iota(jnp.int32, (2 * nj, nj), 1)
    diff = jnp.where(src == dst + 1, 1.0, jnp.where(src == dst - 1, -1.0, 0.0)).astype(jnp.bfloat16)

    def lane_difference(x):
        high = x.astype(jnp.bfloat16)
        low = (x - high.astype(F32)).astype(jnp.bfloat16)
        return jnp.dot(jnp.concatenate([high, low], 1), diff, preferred_element_type=F32)

    tsq[...] = jnp.zeros(tsq.shape, F32)
    for b in range(depth // per):
        here = slice(b * per, (b + 1) * per)
        tsq[0, 0:1, :] = -p_lo[b : b + 1]
        tsq[0, nj - 1 : nj, :] = p_hi[b : b + 1]
        tsq[1, 0:1, :] = -v_lo[b : b + 1]
        tsq[1, nj - 1 : nj, :] = v_hi[b : b + 1]
        p = press[here]
        pe[here, PAD : PAD + ni, :] = p
        p = p.reshape(rows, nj)
        u = zonal[here] - H_STEP * (pe[here, PAD + 1 : PAD + 1 + ni, :] - pe[here, PAD - 1 : PAD - 1 + ni, :])
        zonal_out[here] = u
        ue[here, PAD : PAD + ni, :] = u
        v = merid[here].reshape(rows, nj) - H_STEP * (lane_difference(p) + tsq[0].T)
        merid_out[here] = v.reshape(per, ni, nj)
        spread = (ue[here, PAD + 1 : PAD + 1 + ni, :] - ue[here, PAD - 1 : PAD - 1 + ni, :]).reshape(rows, nj)
        spread = spread + (lane_difference(v) + tsq[1].T)
        part[here] = (p - D_STEP * spread).reshape(per, ni, nj)

    lo = vert[0] - V_STEP * part[1]
    hi = vert[last] + V_STEP * part[last - 1]
    y_out[0], y_out[last] = lo, hi
    for s in range(1, half):
        k, j = s, last - s
        lo = (vert[k] - V_STEP * (part[k + 1] - part[k - 1])) + mul[k] * lo
        hi = (vert[j] - V_STEP * (part[j + 1] - part[j - 1])) + mul[j + 1] * hi
        y_out[k], y_out[j] = lo, hi
    hi = inv[half] * (hi + mul[half] * lo)
    lo = inv[half - 1] * lo + mul[half] * hi
    y_out[half], y_out[half - 1] = hi, lo
    for s in range(1, half):
        k, j = half - 1 - s, half + s
        lo = inv[k] * y_out[k] + mul[k + 1] * lo
        hi = inv[j] * y_out[j] + mul[j] * hi
        y_out[k], y_out[j] = lo, hi
    p_first, p_last = part[0], part[last]
    planes[0], planes[1] = lo, hi
    planes[2], planes[3] = p_first, p_last
    if paired:
        lower = group < 2
        sign = jnp.where(lower, V_STEP, -V_STEP)
        y_near, y_far = jnp.where(lower, hi, lo), jnp.where(lower, lo, hi)
        p_near, p_far = jnp.where(lower, p_last, p_first), jnp.where(lower, p_first, p_last)
        gain = cf[4] * cf[0]
        inside = y_near - gain * (cf[5] * (sign * p_far) + y_far)
        outside = cf[4] * (sign * p_near) + gain * (y_near - cf[6] * (sign * p_near))
        across[0] = jnp.where((group == 1) | (group == 2), inside, outside)
        across[1] = p_near


def paired_sources(group, cf, own, mate, crossed, lv):
    lower = group < 2
    is_inner = (group == 1) | (group == 2)
    sign = jnp.where(lower, V_STEP, -V_STEP)
    near = jnp.where(lower, 1, 0)
    slot = jnp.where(is_inner, 0, 1)
    lv[slot] = own[...]
    lv[1 - slot] = mate[...]
    kappa, mine, other, gain, x, g_out, g_in = (cf[n] for n in range(7))
    y_in_near, y_in_far, y_out = lv[0, near], lv[0, 1 - near], lv[1, near]
    p_in_near = sign * lv[0, 2 + near]
    p_in_far = sign * lv[0, 3 - near]
    p_out = sign * lv[1, 2 + near]
    flux = kappa * ((y_out - g_out * p_in_far) - (y_in_far + g_in * p_out))
    here = y_in_near + x * (p_out + flux)
    there = crossed[0][0] + crossed[1][0]
    p_there = sign * jnp.where(is_inner, crossed[1][1], crossed[0][1])
    middle = gain * ((there - here) + (other * p_in_near + mine * p_there))
    n_here = middle - p_there
    n_there = p_in_near - middle
    flux = flux - kappa * x * n_here
    in_far = p_out + flux
    out_near = -(p_in_far + flux)
    near_source = jnp.where(is_inner, n_here, out_near)
    far_source = jnp.where(is_inner, in_far, 0.0)
    alpha = jnp.where(lower, far_source, near_source)
    beta = jnp.where(lower, near_source, far_source)
    under = jnp.where(
        group == 1,
        y_out + g_out * out_near,
        jnp.where(
            group == 2,
            there + other * n_there,
            jnp.where(group == 3, y_in_far + g_in * in_far + x * n_here, 0.0),
        ),
    )
    return alpha, beta, under


def chain_sources(groups, group, st, own, got, lv):
    lv[group] = own[...]
    for m in range(1, groups):
        lv[source_of(group, m, groups)] = got[m - 1][...]
    zero = jnp.zeros(own.shape[1:], F32)
    z_top, z_bot = [], []
    for g in range(groups):
        below = V_STEP * lv[g - 1, 3] if g else zero
        above = V_STEP * lv[g + 1, 2] if g < groups - 1 else zero
        z_top.append(lv[g, 0] + st[g, 0] * below - st[g, 1] * above)
        z_bot.append(lv[g, 1] + st[g, 1] * below - st[g, 2] * above)
    ratios, parts = [zero], [zero]
    for g in range(1, groups):
        cg = st[g, 3]
        down = cg * st[g - 1, 1]
        pivot = 1.0 / (1.0 + cg * (st[g - 1, 2] + st[g, 0]) - down * ratios[-1])
        parts.append((cg * (z_bot[g - 1] - z_top[g]) + down * parts[-1]) * pivot)
        ratios.append(cg * st[g, 1] * pivot)
    flux = [zero] * (groups + 1)
    for g in range(groups - 1, 0, -1):
        flux[g] = parts[g] + ratios[g] * flux[g + 1]
    alpha, beta, under = zero, zero, zero
    for g in range(groups):
        mine = group == g
        if g:
            alpha = jnp.where(mine, V_STEP * lv[g - 1, 3] + flux[g], alpha)
            bot = z_bot[g - 1] + st[g - 1, 1] * flux[g - 1] - st[g - 1, 2] * flux[g]
            under = jnp.where(mine, bot, under)
        if g < groups - 1:
            beta = jnp.where(mine, -(V_STEP * lv[g + 1, 2] + flux[g + 1]), beta)
    return alpha, beta, under


def finish_kernel(groups, final, hx, hy, where, *refs):
    refs = list(refs)
    take = lambda n: [refs.pop(0) for _ in range(n)]
    y, part, g0, gl, system, own = take(6)
    got = take(groups - 1)
    vert_out, press_out = take(2)
    mx, my = ([], []) if final else (take(hx.count), take(hy.count))
    lv = take(1)[0]
    depth, ni, nj = y.shape
    group = where[0]
    if groups == 4:
        alpha, beta, under = paired_sources(group, system, own, got[0], got[1:], lv)
    else:
        alpha, beta, under = chain_sources(groups, group, system, own, got, lv)

    def level(k, w_prev):
        w = y[k] + g0[k] * alpha + gl[k] * beta
        vert_out[k] = w
        press_out[k] = part[k] - P_STEP * (w - w_prev)
        return w

    lax.fori_loop(0, depth, level, under, unroll=4)
    if final:
        return
    both_x, both_y = take(2)
    pack_pressure(press_out, both_x, both_y)
    hx.write(mx, both_x, where[1] == 0)
    hy.write(my, both_y, where[2] == 0)


def body(zonal, meridional, vertical, pressure, coupling, surface, lid_flag):
    depth, ni, nj = coupling.shape
    full, four, two = (depth, ni, nj), (4, ni, nj), (2, ni, nj)
    groups = lax.axis_size("lev")
    paired = groups == 4
    hx = Halo("gx", (depth, nj))
    hy = Halo("gy", (depth // (nj // ni), nj))
    where = jnp.stack([lax.axis_index("lev"), lax.axis_index("gx") % 2, lax.axis_index("gy") % 2]).astype(jnp.int32)

    results = call(
        functools.partial(first_kernel, hx, hy, groups),
        [full] * 3 + hx.shapes(3) + hy.shapes(3) + [full] * 4 + [four],
        [where, zonal, meridional, pressure, coupling, surface, lid_flag],
        scratch=[
            hx.scratch(3),
            hy.scratch(3),
            pltpu.VMEM(full, F32),
            pltpu.VMEM(surface.shape, surface.dtype),
            pltpu.VMEM(lid_flag.shape, lid_flag.dtype),
            pltpu.SemaphoreType.DMA((6,)),
        ],
        spaces=[SMEM] + [HBM] * 6,
    )
    zonal, meridional, pressure = results[:3]
    ox, oy = results[3 : 3 + hx.count], results[3 + hx.count : 3 + hx.count + hy.count]
    inv, mul, g0, gl, own_s = results[3 + hx.count + hy.count :]
    ry, rx = hy.exchange(oy), hx.exchange(ox)
    got_s = [to_lev(own_s, m) for m in range(1, groups)]
    system = uh = vh = None
    for substep in range(SUBSTEPS):
        first, final = substep == 0, substep == SUBSTEPS - 1
        args = [where, zonal, meridional, vertical, pressure, inv, mul] + ox + oy + rx + ry
        outs = [full] * 4 + [four, (2,) + hx.plane, (2,) + hy.plane]
        if first:
            args += [own_s] + got_s
        else:
            args += [uh, vh] + ([system] if paired else [])
        if paired:
            outs += [two]
        if first:
            outs += [(groups, 4, ni, nj)] + ([(7, ni, nj)] if paired else [])
        results = call(
            functools.partial(advance_kernel, first, hx, hy, groups),
            outs,
            args,
            scratch=[
                pltpu.VMEM((depth, ni + 2 * PAD, nj), F32),
                pltpu.VMEM((depth, ni + 2 * PAD, nj), F32),
                pltpu.VMEM((2, nj, nj), F32),
            ],
        )
        zonal, meridional, y, part, own, uh, vh = results[:7]
        if first:
            system = results[-1]
        if paired:
            across = results[7]
            got = [to_lev(own, 1), to_lev(across, 2), to_lev(across, 3)]
        else:
            got = [to_lev(own, m) for m in range(1, groups)]
        outs, scratch = [full, full], [pltpu.VMEM((groups, 4, ni, nj), F32)]
        if not final:
            outs += hx.shapes(2) + hy.shapes(2)
            scratch += [hx.scratch(2), hy.scratch(2)]
        results = call(
            functools.partial(finish_kernel, groups, final, hx, hy),
            outs,
            [where, y, part, g0, gl, system, own] + got,
            scratch=scratch,
        )
        vertical, pressure = results[:2]
        if not final:
            ox, oy = results[2 : 2 + hx.count], results[2 + hx.count :]
            ry, rx = hy.exchange(oy), hx.exchange(ox)
    return (zonal, meridional, vertical, pressure)


def solution(mesh):
    block = P("lev", "gx", "gy")
    plane = P("gx", "gy")
    return jax.shard_map(
        body,
        mesh=mesh,
        in_specs=(block,) * 5 + (plane,) * 2,
        out_specs=(block,) * 4,
        check_vma=False,
    )
```

```python
import functools

import jax
import jax.numpy as jnp
from jax import lax
from jax.experimental import pallas as pl
from jax.experimental.pallas import tpu as pltpu
from jax.sharding import PartitionSpec as P

SUBSTEPS = 3
H_STEP = 0.25
D_STEP = 0.25
V_STEP = 0.5
P_STEP = 0.5
F32 = jnp.float32
PAD = 8

VMEM = pl.BlockSpec(memory_space=pltpu.VMEM)
HBM = pl.BlockSpec(memory_space=pltpu.HBM)


def call(kernel, outs, args, scratch=(), spaces=None, out_spaces=None, types=()):
    return list(
        pl.pallas_call(
            kernel,
            out_shape=[jax.ShapeDtypeStruct(s, types[n] if n < len(types) else F32) for n, s in enumerate(outs)],
            in_specs=spaces or [VMEM] * len(args),
            out_specs=out_spaces or [VMEM] * len(outs),
            scratch_shapes=list(scratch),
            compiler_params=pltpu.CompilerParams(vmem_limit_bytes=20 * 1024 * 1024),
        )(*args)
    )


class Halo:
    def __init__(self, axis, plane):
        self.axis, self.plane = axis, plane
        self.n = lax.axis_size(axis)
        self.count = 1 if self.n <= 2 else 2
        self.swap = self.n > 2 and self.n % 2 == 0

    def shapes(self, rows):
        return [(2 * rows,) + self.plane] if self.count == 1 else [(rows,) + self.plane] * 2

    def scratch(self, rows):
        return pltpu.VMEM((2, rows) + self.plane, F32)

    def write(self, refs, both, even):
        rows = both.shape[1]
        if self.count == 1:
            refs[0][:rows] = both[0]
            refs[0][rows:] = both[1]
        elif self.swap:
            refs[0][...] = jnp.where(even, both[0], both[1])
            refs[1][...] = jnp.where(even, both[1], both[0])
        else:
            refs[0][...] = both[0]
            refs[1][...] = both[1]

    def up(self, refs, r, even):
        if self.swap:
            return jnp.where(even, refs[0][r], refs[1][r])
        return refs[0][r]

    def down(self, refs, r, even):
        if self.swap:
            return jnp.where(even, refs[1][r], refs[0][r])
        return refs[0][refs[0].shape[0] // 2 + r] if self.count == 1 else refs[1][r]

    def low(self, refs, r, even):
        if self.swap:
            return jnp.where(even, refs[1][r], refs[0][r])
        return refs[0][r]

    def high(self, refs, r, even):
        if self.swap:
            return jnp.where(even, refs[0][r], refs[1][r])
        return refs[0][refs[0].shape[0] // 2 + r] if self.count == 1 else refs[1][r]

    def exchange(self, messages):
        n = self.n
        if n == 1:
            return messages
        if self.swap:
            first = [(i, i ^ 1) for i in range(n)]
            second = [(i, (i + 1) % n if i % 2 else (i - 1) % n) for i in range(n)]
            got = lax.ppermute(messages[1], self.axis, second)
            return [lax.ppermute(messages[0], self.axis, first), got]
        up = [(i, (i + 1) % n) for i in range(n)]
        if n == 2:
            return [lax.ppermute(messages[0], self.axis, up)]
        down = [(j, i) for i, j in up]
        return [lax.ppermute(messages[0], self.axis, up), lax.ppermute(messages[1], self.axis, down)]


def to_lev(message, m):
    n = lax.axis_size("lev")
    if n & (n - 1) == 0:
        return lax.ppermute(message, "lev", [(i, i ^ m) for i in range(n)])
    return lax.ppermute(message, "lev", [(i, (i + m) % n) for i in range(n)])


def source_of(group, m, n):
    return group ^ m if n & (n - 1) == 0 else (group - m) % n


def pack_columns(ref, picks, outs):
    depth, ni, nj = ref.shape
    per = nj // ni
    for b in range(depth // per):
        turned = ref[b * per : (b + 1) * per].reshape(per * ni, nj).T
        for c, out in zip(picks, outs):
            out[b : b + 1, :] = turned[c : c + 1, :]


def pack_pressure(press, both_x, both_y):
    ni, nj = press.shape[1:]
    for r in range(2):
        both_x[0, r] = press[:, ni - 2 + r, :]
        both_x[1, r] = press[:, r, :]
    pack_columns(press, (nj - 2, nj - 1, 0, 1), (both_y.at[0, 0], both_y.at[0, 1], both_y.at[1, 0], both_y.at[1, 1]))


def first_kernel(hx, hy, *refs):
    refs = list(refs)
    take = lambda n: [refs.pop(0) for _ in range(n)]
    sources, targets = take(6), take(6)
    mx, my = take(hx.count), take(hy.count)
    both_x, both_y, sems = refs
    p, v, u = targets[:3]
    copies = [pltpu.make_async_copy(a, b, sems.at[n]) for n, (a, b) in enumerate(zip(sources, targets))]
    for copy in copies:
        copy.start()
    ni, nj = p.shape[1:]
    copies[0].wait()
    pack_pressure(p, both_x, both_y)
    copies[1].wait()
    pack_columns(v, (nj - 1, 0), (both_y.at[0, 2], both_y.at[1, 2]))
    copies[2].wait()
    both_x[0, 2] = u[:, ni - 1, :]
    both_x[1, 2] = u[:, 0, :]
    hx.write(mx, both_x, lax.axis_index("gx") % 2 == 0)
    hy.write(my, both_y, lax.axis_index("gy") % 2 == 0)
    for copy in copies[3:]:
        copy.wait()


def factor_kernel(groups, c, surface, lid, inv, mul, g0, gl, planes):
    depth, ni, nj = c.shape
    last, half = depth - 1, depth // 2
    group = lax.axis_index("lev")
    bottom = group == 0
    top = group == groups - 1
    ground = surface[...] - group * depth
    lidf = jnp.where(top, lid[...].astype(F32), 0.0)

    def coupling(k):
        return jnp.where(ground <= k - 1, c[k], 0.0)

    def diag(k):
        low = c[k] if k > 0 else jnp.where(bottom, c[k], 0.0)
        high = c[k + 1] if k < last else lidf * c[k]
        return 1.0 + low + high

    lo, hi = None, None
    for s in range(half):
        k, j = s, last - s
        d_lo, d_hi = diag(k), diag(j)
        if s:
            e_lo = coupling(k)
            m_lo = e_lo * lo
            mul[k] = m_lo
            d_lo = d_lo - e_lo * m_lo
            e_hi = coupling(j + 1)
            m_hi = e_hi * hi
            mul[j + 1] = m_hi
            d_hi = d_hi - e_hi * m_hi
        if j == half:
            e_mid = coupling(half)
            lo = jnp.where(ground <= k, 1.0 / d_lo, 0.0)
            m_mid = e_mid * lo
            mul[half] = m_mid
            d_hi = d_hi - e_mid * m_mid
        else:
            lo = jnp.where(ground <= k, 1.0 / d_lo, 0.0)
        hi = jnp.where(ground <= j, 1.0 / d_hi, 0.0)
        inv[k] = lo
        inv[j] = hi
    one = jnp.ones((ni, nj), F32)
    t0 = [one] + [None] * (half - 1)
    tl = [one] + [None] * (half - 1)
    for s in range(1, half):
        t0[s] = mul[s] * t0[s - 1]
        tl[s] = mul[last - s + 1] * tl[s - 1]
        g0[s] = t0[s]
        gl[last - s] = tl[s]
    g0[0] = one
    gl[last] = one
    xh0 = inv[half] * (mul[half] * t0[half - 1])
    xhl = inv[half] * tl[half - 1]
    xk0 = inv[half - 1] * t0[half - 1] + mul[half] * xh0
    xkl = mul[half] * xhl
    g0[half], gl[half] = xh0, xhl
    g0[half - 1], gl[half - 1] = xk0, xkl
    for s in range(1, half):
        k, j = half - 1 - s, half + s
        xk0 = inv[k] * g0[k] + mul[k + 1] * xk0
        xkl = mul[k + 1] * xkl
        xh0 = mul[j] * xh0
        xhl = inv[j] * gl[j] + mul[j] * xhl
        g0[k], gl[k] = xk0, xkl
        g0[j], gl[j] = xh0, xhl
    planes[0] = g0[0]
    planes[1] = g0[last]
    planes[2] = gl[last]
    planes[3] = c[0]


def condense(group, st, cf):
    half = group // 2
    near = jnp.where(half == 0, 2, 0)
    inner = 1 + half
    outer = 3 * half

    def half_of(inner, outer, near):
        odd = jnp.where(inner == 1, 1, 3)
        c = st[odd, 3]
        x = st[inner, 1]
        kappa = c / (1.0 + c * (st[outer, near] + st[inner, 2 - near]))
        return kappa, st[inner, near] - kappa * x * x, x

    kappa, mine, x = half_of(inner, outer, near)
    _, other, _ = half_of(3 - inner, 3 - outer, 2 - near)
    c = st[2, 3]
    cf[0] = kappa
    cf[1] = mine
    cf[2] = other
    cf[3] = c / (1.0 + c * (mine + other))
    cf[4] = x
    cf[5] = st[outer, near]
    cf[6] = st[inner, 2 - near]


def spread_setup(groups, group, own, got, st):
    st[group] = own[...]
    for m in range(1, groups):
        st[source_of(group, m, groups)] = got[m - 1][...]


def lane_matrix(nj):
    src = lax.broadcasted_iota(jnp.int32, (2 * nj, nj), 0) % nj
    dst = lax.broadcasted_iota(jnp.int32, (2 * nj, nj), 1)
    return jnp.where(src == dst + 1, 1.0, jnp.where(src == dst - 1, -1.0, 0.0)).astype(jnp.bfloat16)


def lane_difference(x, matrix):
    high = x.astype(jnp.bfloat16)
    low = (x - high.astype(F32)).astype(jnp.bfloat16)
    return jnp.dot(jnp.concatenate([high, low], 1), matrix, preferred_element_type=F32)


def add_rows(ref, rows):
    for r, plane in rows:
        ref[:, r, :] = ref[:, r, :] + plane


def interior_kernel(first, *refs):
    refs = list(refs)
    take = lambda n: [refs.pop(0) for _ in range(n)]
    zonal, merid, press = take(3)
    uc, vc = (None, None) if first else take(2)
    zonal_out, merid_out, part = take(3)
    pe, ue, square = take(3)
    depth, ni, nj = press.shape
    per = nj // ni
    rows = per * ni
    matrix = lane_matrix(nj)
    edge = jnp.zeros((depth, nj), F32)
    for ref in (pe, ue):
        ref[:, PAD - 1, :] = edge
        ref[:, PAD + ni, :] = edge
    above, below = slice(PAD + 1, PAD + 1 + ni), slice(PAD - 1, PAD - 1 + ni)
    if not first:
        square[...] = jnp.zeros(square.shape, F32)
    for b in range(depth // per):
        here = slice(b * per, (b + 1) * per)
        pe[here, PAD : PAD + ni, :] = press[here]
        zonal_out[here] = zonal[here] - H_STEP * (pe[here, above, :] - pe[here, below, :])
    if not first:
        add_rows(zonal_out, ((0, uc[0]), (ni - 1, uc[1])))
    for b in range(depth // per):
        here = slice(b * per, (b + 1) * per)
        p = press[here].reshape(rows, nj)
        ue[here, PAD : PAD + ni, :] = zonal_out[here]
        v = merid[here].reshape(rows, nj)
        if not first:
            square[0:1, :] = vc[0, b : b + 1, :]
            square[nj - 1 : nj, :] = vc[1, b : b + 1, :]
            v = v + square[...].T
        v = v - H_STEP * lane_difference(p, matrix)
        merid_out[here] = v.reshape(per, ni, nj)
        spread = (ue[here, above, :] - ue[here, below, :]).reshape(rows, nj) + lane_difference(v, matrix)
        part[here] = (p - D_STEP * spread).reshape(per, ni, nj)


def emit_kernel(zonal, merid, uc, vc, zonal_out, merid_out, square):
    depth, ni, nj = zonal.shape
    per = nj // ni
    square[...] = jnp.zeros(square.shape, F32)
    for b in range(depth // per):
        here = slice(b * per, (b + 1) * per)
        square[0:1, :] = vc[0, b : b + 1, :]
        square[nj - 1 : nj, :] = vc[1, b : b + 1, :]
        merid_out[here] = merid[here] + square[...].T.reshape(per, ni, nj)
        zonal_out[here] = zonal[here]
    add_rows(zonal_out, ((0, uc[0]), (ni - 1, uc[1])))


def solve_kernel(first, hx, hy, groups, *refs):
    refs = list(refs)
    take = lambda n: [refs.pop(0) for _ in range(n)]
    paired = groups == 4 and not first
    part0, vert, inv, mul = take(4)
    ox, oy = take(hx.count), take(hy.count)
    rx, ry = take(hx.count), take(hy.count)
    uh, vh = (None, None) if first else take(2)
    cf = take(1)[0] if paired else None
    y_out, part, planes, uh_out, vh_out, uc, vc = take(7)
    across = take(1)[0] if paired else None
    square = take(1)[0]
    depth, ni, nj = part0.shape
    last, half, per = depth - 1, depth // 2, nj // ni
    group = lax.axis_index("lev")
    even_x, even_y = lax.axis_index("gx") % 2 == 0, lax.axis_index("gy") % 2 == 0

    u_lo = hx.low(rx, 2, even_x) if first else uh[0]
    u_hi = hx.high(rx, 2, even_x) if first else uh[1]
    u_lo = u_lo - H_STEP * (hx.down(ox, 0, even_x) - hx.low(rx, 0, even_x))
    u_hi = u_hi - H_STEP * (hx.high(rx, 1, even_x) - hx.up(ox, 1, even_x))
    uh_out[0], uh_out[1] = u_lo, u_hi
    u_first, u_last = H_STEP * hx.low(rx, 1, even_x), -H_STEP * hx.high(rx, 0, even_x)
    uc[0], uc[1] = u_first, u_last
    v_lo = hy.low(ry, 2, even_y) if first else vh[0]
    v_hi = hy.high(ry, 2, even_y) if first else vh[1]
    v_lo = v_lo - H_STEP * (hy.down(oy, 0, even_y) - hy.low(ry, 0, even_y))
    v_hi = v_hi - H_STEP * (hy.high(ry, 1, even_y) - hy.up(oy, 1, even_y))
    vh_out[0], vh_out[1] = v_lo, v_hi
    v_first, v_last = H_STEP * hy.low(ry, 1, even_y), -H_STEP * hy.high(ry, 0, even_y)
    vc[0], vc[1] = v_first, v_last
    square[...] = jnp.zeros(square.shape, F32)
    for b in range(depth // per):
        here = slice(b * per, (b + 1) * per)
        one = slice(b, b + 1)
        square[0:1, :] = D_STEP * v_lo[one]
        square[1:2, :] = D_STEP * v_first[one]
        square[nj - 2 : nj - 1, :] = -D_STEP * v_last[one]
        square[nj - 1 : nj, :] = -D_STEP * v_hi[one]
        part[here] = part0[here] + square[...].T.reshape(per, ni, nj)
    edges = ((0, D_STEP * u_lo), (1, D_STEP * u_first), (ni - 2, -D_STEP * u_last), (ni - 1, -D_STEP * u_hi))
    add_rows(part, edges)

    lo = vert[0] - V_STEP * part[1]
    hi = vert[last] + V_STEP * part[last - 1]
    y_out[0], y_out[last] = lo, hi
    for s in range(1, half):
        k, j = s, last - s
        lo = (vert[k] - V_STEP * (part[k + 1] - part[k - 1])) + mul[k] * lo
        hi = (vert[j] - V_STEP * (part[j + 1] - part[j - 1])) + mul[j + 1] * hi
        y_out[k], y_out[j] = lo, hi
    hi = inv[half] * (hi + mul[half] * lo)
    lo = inv[half - 1] * lo + mul[half] * hi
    y_out[half], y_out[half - 1] = hi, lo
    for s in range(1, half):
        k, j = half - 1 - s, half + s
        lo = inv[k] * y_out[k] + mul[k + 1] * lo
        hi = inv[j] * y_out[j] + mul[j] * hi
        y_out[k], y_out[j] = lo, hi
    p_first, p_last = part[0], part[last]
    planes[0], planes[1] = lo, hi
    planes[2], planes[3] = p_first, p_last
    if paired:
        lower = group < 2
        sign = jnp.where(lower, V_STEP, -V_STEP)
        y_near, y_far = jnp.where(lower, hi, lo), jnp.where(lower, lo, hi)
        p_near, p_far = jnp.where(lower, p_last, p_first), jnp.where(lower, p_first, p_last)
        gain = cf[4] * cf[0]
        inside = y_near - gain * (cf[5] * (sign * p_far) + y_far)
        outside = cf[4] * (sign * p_near) + gain * (y_near - cf[6] * (sign * p_near))
        across[0] = jnp.where((group == 1) | (group == 2), inside, outside)
        across[1] = p_near


def paired_sources(group, cf, own, mate, crossed, lv):
    lower = group < 2
    is_inner = (group == 1) | (group == 2)
    sign = jnp.where(lower, V_STEP, -V_STEP)
    near = jnp.where(lower, 1, 0)
    slot = jnp.where(is_inner, 0, 1)
    lv[slot] = own[...]
    lv[1 - slot] = mate[...]
    kappa, mine, other, gain, x, g_out, g_in = (cf[n] for n in range(7))
    y_in_near, y_in_far, y_out = lv[0, near], lv[0, 1 - near], lv[1, near]
    p_in_near = sign * lv[0, 2 + near]
    p_in_far = sign * lv[0, 3 - near]
    p_out = sign * lv[1, 2 + near]
    flux = kappa * ((y_out - g_out * p_in_far) - (y_in_far + g_in * p_out))
    here = y_in_near + x * (p_out + flux)
    there = crossed[0][0] + crossed[1][0]
    p_there = sign * jnp.where(is_inner, crossed[1][1], crossed[0][1])
    middle = gain * ((there - here) + (other * p_in_near + mine * p_there))
    n_here = middle - p_there
    n_there = p_in_near - middle
    flux = flux - kappa * x * n_here
    in_far = p_out + flux
    out_near = -(p_in_far + flux)
    near_source = jnp.where(is_inner, n_here, out_near)
    far_source = jnp.where(is_inner, in_far, 0.0)
    alpha = jnp.where(lower, far_source, near_source)
    beta = jnp.where(lower, near_source, far_source)
    under = jnp.where(
        group == 1,
        y_out + g_out * out_near,
        jnp.where(
            group == 2,
            there + other * n_there,
            jnp.where(group == 3, y_in_far + g_in * in_far + x * n_here, 0.0),
        ),
    )
    return alpha, beta, under


def chain_sources(groups, group, st, own, got, lv):
    lv[group] = own[...]
    for m in range(1, groups):
        lv[source_of(group, m, groups)] = got[m - 1][...]
    zero = jnp.zeros(own.shape[1:], F32)
    z_top, z_bot = [], []
    for g in range(groups):
        below = V_STEP * lv[g - 1, 3] if g else zero
        above = V_STEP * lv[g + 1, 2] if g < groups - 1 else zero
        z_top.append(lv[g, 0] + st[g, 0] * below - st[g, 1] * above)
        z_bot.append(lv[g, 1] + st[g, 1] * below - st[g, 2] * above)
    ratios, parts = [zero], [zero]
    for g in range(1, groups):
        cg = st[g, 3]
        down = cg * st[g - 1, 1]
        pivot = 1.0 / (1.0 + cg * (st[g - 1, 2] + st[g, 0]) - down * ratios[-1])
        parts.append((cg * (z_bot[g - 1] - z_top[g]) + down * parts[-1]) * pivot)
        ratios.append(cg * st[g, 1] * pivot)
    flux = [zero] * (groups + 1)
    for g in range(groups - 1, 0, -1):
        flux[g] = parts[g] + ratios[g] * flux[g + 1]
    alpha, beta, under = zero, zero, zero
    for g in range(groups):
        mine = group == g
        if g:
            alpha = jnp.where(mine, V_STEP * lv[g - 1, 3] + flux[g], alpha)
            bot = z_bot[g - 1] + st[g - 1, 1] * flux[g - 1] - st[g - 1, 2] * flux[g]
            under = jnp.where(mine, bot, under)
        if g < groups - 1:
            beta = jnp.where(mine, -(V_STEP * lv[g + 1, 2] + flux[g + 1]), beta)
    return alpha, beta, under


def finish_kernel(groups, first, final, hx, hy, *refs):
    refs = list(refs)
    take = lambda n: [refs.pop(0) for _ in range(n)]
    y, part, g0, gl, own = take(5)
    got = take(groups - 1)
    paired = groups == 4 and not first
    if first:
        own_s, got_s = take(1)[0], take(groups - 1)
    else:
        system = take(1)[0]
    vert_out, press_out = take(2)
    mx, my = ([], []) if final else (take(hx.count), take(hy.count))
    if first:
        system = take(1)[0]
        st = take(1)[0] if groups == 4 else system
    lv = take(1)[0]
    depth, ni, nj = y.shape
    group = lax.axis_index("lev")
    if first:
        spread_setup(groups, group, own_s, got_s, st)
        alpha, beta, under = chain_sources(groups, group, st, own, got, lv)
        if groups == 4:
            condense(group, st, system)
    elif paired:
        alpha, beta, under = paired_sources(group, system, own, got[0], got[1:], lv)
    else:
        alpha, beta, under = chain_sources(groups, group, system, own, got, lv)
    vert, press = take(2) if final else (vert_out, press_out)

    def level(k, w_prev):
        w = y[k] + g0[k] * alpha + gl[k] * beta
        vert[k] = w
        press[k] = part[k] - P_STEP * (w - w_prev)
        return w

    if final:
        sems = take(1)[0]
        step, w, copies = max(depth // 4, 1), under, []
        for start in range(0, depth, step):
            stop = min(start + step, depth)
            w = lax.fori_loop(start, stop, level, w, unroll=True)
            for n, (a, b) in enumerate(((vert, vert_out), (press, press_out))):
                here = pl.ds(start, stop - start)
                copies.append(pltpu.make_async_copy(a.at[here], b.at[here], sems.at[n, start // step]))
                copies[-1].start()
        for copy in copies:
            copy.wait()
        return
    lax.fori_loop(0, depth, level, under, unroll=4)
    both_x, both_y = take(2)
    pack_pressure(press_out, both_x, both_y)
    hx.write(mx, both_x, lax.axis_index("gx") % 2 == 0)
    hy.write(my, both_y, lax.axis_index("gy") % 2 == 0)


def body(zonal, meridional, vertical, pressure, coupling, surface, lid_flag):
    depth, ni, nj = coupling.shape
    full, four, two = (depth, ni, nj), (4, ni, nj), (2, ni, nj)
    groups = lax.axis_size("lev")
    hx = Halo("gx", (depth, nj))
    hy = Halo("gy", (depth // (nj // ni), nj))
    wide = pltpu.VMEM((depth, ni + 2 * PAD, nj), F32)
    square = pltpu.VMEM((nj, nj), F32)

    inputs = (pressure, meridional, zonal, coupling, surface, lid_flag)
    results = call(
        functools.partial(first_kernel, hx, hy),
        [full] * 4 + [surface.shape] * 2 + hx.shapes(3) + hy.shapes(3),
        [pltpu.with_memory_space_constraint(a, pltpu.HBM) for a in inputs],
        scratch=[hx.scratch(3), hy.scratch(3), pltpu.SemaphoreType.DMA((6,))],
        spaces=[HBM] * 6,
        types=[a.dtype for a in inputs],
    )
    pressure, meridional, zonal, coupling, surface, lid_flag = results[:6]
    ox, oy = results[6 : 6 + hx.count], results[6 + hx.count :]
    ry, rx = hy.exchange(oy), hx.exchange(ox)
    inv, mul, g0, gl, own_s = call(
        functools.partial(factor_kernel, groups), [full] * 4 + [four], [coupling, surface, lid_flag]
    )
    got_s = [to_lev(own_s, m) for m in range(1, groups)]
    system = uh = vh = uc = vc = None
    for substep in range(SUBSTEPS):
        first, final = substep == 0, substep == SUBSTEPS - 1
        paired = groups == 4 and not first
        args = [zonal, meridional, pressure] + ([] if first else [uc, vc])
        zonal, meridional, part = call(
            functools.partial(interior_kernel, first), [full] * 3, args, scratch=[wide, wide, square]
        )
        args = [part, vertical, inv, mul] + ox + oy + rx + ry
        args += ([] if first else [uh, vh]) + ([system] if paired else [])
        outs = [full, full, four] + [(2,) + hx.plane, (2,) + hy.plane] * 2 + ([two] if paired else [])
        results = call(functools.partial(solve_kernel, first, hx, hy, groups), outs, args, scratch=[square])
        y, part, own, uh, vh, uc, vc = results[:7]
        if paired:
            got = [to_lev(own, 1), to_lev(results[7], 2), to_lev(results[7], 3)]
        else:
            got = [to_lev(own, m) for m in range(1, groups)]
        if final:
            zonal, meridional = call(emit_kernel, [full] * 2, [zonal, meridional, uc, vc], scratch=[square])
        args = [y, part, g0, gl, own] + got + ([own_s] + got_s if first else [system])
        outs, scratch = [full, full], []
        if not final:
            outs += hx.shapes(2) + hy.shapes(2)
        if first:
            setup = (groups, 4, ni, nj)
            outs += [(7, ni, nj) if groups == 4 else setup]
            scratch += [pltpu.VMEM(setup, F32)] if groups == 4 else []
        scratch += [pltpu.VMEM((groups, 4, ni, nj), F32)]
        if final:
            scratch += [pltpu.VMEM(full, F32)] * 2 + [pltpu.SemaphoreType.DMA((2, 4))]
        else:
            scratch += [hx.scratch(2), hy.scratch(2)]
        results = call(
            functools.partial(finish_kernel, groups, first, final, hx, hy),
            outs,
            args,
            scratch=scratch,
            out_spaces=[HBM] * 2 if final else None,
        )
        vertical, pressure = results[:2]
        if first:
            system = results[-1]
        if not final:
            ox, oy = results[2 : 2 + hx.count], results[2 + hx.count : 2 + hx.count + hy.count]
            ry, rx = hy.exchange(oy), hx.exchange(ox)
    return (zonal, meridional, vertical, pressure)


def solution(mesh):
    block = P("lev", "gx", "gy")
    plane = P("gx", "gy")
    return jax.shard_map(
        body,
        mesh=mesh,
        in_specs=(block,) * 5 + (plane,) * 2,
        out_specs=(block,) * 4,
        check_vma=False,
    )
```

```python
import functools

import jax
import jax.numpy as jnp
from jax import lax
from jax.experimental import pallas as pl
from jax.experimental.pallas import tpu as pltpu
from jax.sharding import PartitionSpec as P

SUBSTEPS = 3
H_STEP = 0.25
D_STEP = 0.25
V_STEP = 0.5
P_STEP = 0.5
F32 = jnp.float32
PAD = 8

VMEM = pl.BlockSpec(memory_space=pltpu.VMEM)
HBM = pl.BlockSpec(memory_space=pltpu.HBM)


def call(kernel, outs, args, scratch=(), spaces=None, out_spaces=None, types=()):
    return list(
        pl.pallas_call(
            kernel,
            out_shape=[jax.ShapeDtypeStruct(s, types[n] if n < len(types) else F32) for n, s in enumerate(outs)],
            in_specs=spaces or [VMEM] * len(args),
            out_specs=out_spaces or [VMEM] * len(outs),
            scratch_shapes=list(scratch),
            compiler_params=pltpu.CompilerParams(vmem_limit_bytes=20 * 1024 * 1024),
        )(*args)
    )


class Halo:
    def __init__(self, axis, plane):
        self.axis, self.plane = axis, plane
        self.n = lax.axis_size(axis)
        self.count = 1 if self.n <= 2 else 2
        self.swap = self.n > 2 and self.n % 2 == 0

    def shapes(self, rows):
        return [(2 * rows,) + self.plane] if self.count == 1 else [(rows,) + self.plane] * 2

    def scratch(self, rows):
        return pltpu.VMEM((2, rows) + self.plane, F32)

    def write(self, refs, both, even):
        rows = both.shape[1]
        if self.count == 1:
            refs[0][:rows] = both[0]
            refs[0][rows:] = both[1]
        elif self.swap:
            refs[0][...] = jnp.where(even, both[0], both[1])
            refs[1][...] = jnp.where(even, both[1], both[0])
        else:
            refs[0][...] = both[0]
            refs[1][...] = both[1]

    def up(self, refs, r, even):
        if self.swap:
            return jnp.where(even, refs[0][r], refs[1][r])
        return refs[0][r]

    def down(self, refs, r, even):
        if self.swap:
            return jnp.where(even, refs[1][r], refs[0][r])
        return refs[0][refs[0].shape[0] // 2 + r] if self.count == 1 else refs[1][r]

    def low(self, refs, r, even):
        if self.swap:
            return jnp.where(even, refs[1][r], refs[0][r])
        return refs[0][r]

    def high(self, refs, r, even):
        if self.swap:
            return jnp.where(even, refs[0][r], refs[1][r])
        return refs[0][refs[0].shape[0] // 2 + r] if self.count == 1 else refs[1][r]

    def exchange(self, messages):
        n = self.n
        if n == 1:
            return messages
        if self.swap:
            first = [(i, i ^ 1) for i in range(n)]
            second = [(i, (i + 1) % n if i % 2 else (i - 1) % n) for i in range(n)]
            got = lax.ppermute(messages[1], self.axis, second)
            return [lax.ppermute(messages[0], self.axis, first), got]
        up = [(i, (i + 1) % n) for i in range(n)]
        if n == 2:
            return [lax.ppermute(messages[0], self.axis, up)]
        down = [(j, i) for i, j in up]
        return [lax.ppermute(messages[0], self.axis, up), lax.ppermute(messages[1], self.axis, down)]


def to_lev(message, m):
    n = lax.axis_size("lev")
    if n & (n - 1) == 0:
        return lax.ppermute(message, "lev", [(i, i ^ m) for i in range(n)])
    return lax.ppermute(message, "lev", [(i, (i + m) % n) for i in range(n)])


def source_of(group, m, n):
    return group ^ m if n & (n - 1) == 0 else (group - m) % n


def pack_columns(ref, picks, outs):
    depth, ni, nj = ref.shape
    per = nj // ni
    for b in range(depth // per):
        turned = ref[b * per : (b + 1) * per].reshape(per * ni, nj).T
        for c, out in zip(picks, outs):
            out[b : b + 1, :] = turned[c : c + 1, :]


def pack_pressure(press, both_x, both_y):
    ni, nj = press.shape[1:]
    for r in range(2):
        both_x[0, r] = press[:, ni - 2 + r, :]
        both_x[1, r] = press[:, r, :]
    pack_columns(press, (nj - 2, nj - 1, 0, 1), (both_y.at[0, 0], both_y.at[0, 1], both_y.at[1, 0], both_y.at[1, 1]))


def first_kernel(hx, hy, *refs):
    refs = list(refs)
    take = lambda n: [refs.pop(0) for _ in range(n)]
    sources, targets = take(6), take(6)
    mx, my = take(hx.count), take(hy.count)
    both_x, both_y, sems = refs
    p, v, u = targets[:3]
    copies = [pltpu.make_async_copy(a, b, sems.at[n]) for n, (a, b) in enumerate(zip(sources, targets))]
    for copy in copies:
        copy.start()
    ni, nj = p.shape[1:]
    copies[0].wait()
    pack_pressure(p, both_x, both_y)
    copies[1].wait()
    pack_columns(v, (nj - 1, 0), (both_y.at[0, 2], both_y.at[1, 2]))
    copies[2].wait()
    both_x[0, 2] = u[:, ni - 1, :]
    both_x[1, 2] = u[:, 0, :]
    hx.write(mx, both_x, lax.axis_index("gx") % 2 == 0)
    hy.write(my, both_y, lax.axis_index("gy") % 2 == 0)
    for copy in copies[3:]:
        copy.wait()


def factor_kernel(groups, c, surface, lid, inv, mul, g0, gl, planes):
    depth, ni, nj = c.shape
    last, half = depth - 1, depth // 2
    group = lax.axis_index("lev")
    bottom = group == 0
    top = group == groups - 1
    ground = surface[...] - group * depth
    lidf = jnp.where(top, lid[...].astype(F32), 0.0)

    def coupling(k):
        return jnp.where(ground <= k - 1, c[k], 0.0)

    def diag(k):
        low = c[k] if k > 0 else jnp.where(bottom, c[k], 0.0)
        high = c[k + 1] if k < last else lidf * c[k]
        return 1.0 + low + high

    lo, hi = None, None
    for s in range(half):
        k, j = s, last - s
        d_lo, d_hi = diag(k), diag(j)
        if s:
            e_lo = coupling(k)
            m_lo = e_lo * lo
            mul[k] = m_lo
            d_lo = d_lo - e_lo * m_lo
            e_hi = coupling(j + 1)
            m_hi = e_hi * hi
            mul[j + 1] = m_hi
            d_hi = d_hi - e_hi * m_hi
        if j == half:
            e_mid = coupling(half)
            lo = jnp.where(ground <= k, 1.0 / d_lo, 0.0)
            m_mid = e_mid * lo
            mul[half] = m_mid
            d_hi = d_hi - e_mid * m_mid
        else:
            lo = jnp.where(ground <= k, 1.0 / d_lo, 0.0)
        hi = jnp.where(ground <= j, 1.0 / d_hi, 0.0)
        inv[k] = lo
        inv[j] = hi
    one = jnp.ones((ni, nj), F32)
    t0 = [one] + [None] * (half - 1)
    tl = [one] + [None] * (half - 1)
    for s in range(1, half):
        t0[s] = mul[s] * t0[s - 1]
        tl[s] = mul[last - s + 1] * tl[s - 1]
        g0[s] = t0[s]
        gl[last - s] = tl[s]
    g0[0] = one
    gl[last] = one
    xh0 = inv[half] * (mul[half] * t0[half - 1])
    xhl = inv[half] * tl[half - 1]
    xk0 = inv[half - 1] * t0[half - 1] + mul[half] * xh0
    xkl = mul[half] * xhl
    g0[half], gl[half] = xh0, xhl
    g0[half - 1], gl[half - 1] = xk0, xkl
    for s in range(1, half):
        k, j = half - 1 - s, half + s
        xk0 = inv[k] * g0[k] + mul[k + 1] * xk0
        xkl = mul[k + 1] * xkl
        xh0 = mul[j] * xh0
        xhl = inv[j] * gl[j] + mul[j] * xhl
        g0[k], gl[k] = xk0, xkl
        g0[j], gl[j] = xh0, xhl
    planes[0] = g0[0]
    planes[1] = g0[last]
    planes[2] = gl[last]
    planes[3] = c[0]


def condense(group, own, mate, cf):
    lower = group < 2
    is_inner = (group == 1) | (group == 2)
    inner = [jnp.where(is_inner, own[n], mate[n]) for n in range(4)]
    outer = [jnp.where(is_inner, mate[n], own[n]) for n in range(4)]
    x = inner[1]
    g_out, g_in = jnp.where(lower, outer[2], outer[0]), jnp.where(lower, inner[0], inner[2])
    c = jnp.where(lower, inner[3], outer[3])
    kappa = c / (1.0 + c * (g_out + g_in))
    cf[0] = kappa
    cf[1] = jnp.where(lower, inner[2], inner[0]) - kappa * x * x
    cf[2] = jnp.zeros_like(x)
    cf[3] = jnp.zeros_like(x)
    cf[4] = x
    cf[5] = g_out
    cf[6] = g_in
    cf[7] = inner[3]


def spread_setup(groups, group, own, got, st):
    st[group] = own[...]
    for m in range(1, groups):
        st[source_of(group, m, groups)] = got[m - 1][...]


def lane_matrix(nj):
    src = lax.broadcasted_iota(jnp.int32, (2 * nj, nj), 0) % nj
    dst = lax.broadcasted_iota(jnp.int32, (2 * nj, nj), 1)
    return jnp.where(src == dst + 1, 1.0, jnp.where(src == dst - 1, -1.0, 0.0)).astype(jnp.bfloat16)


def lane_difference(x, matrix):
    high = x.astype(jnp.bfloat16)
    low = (x - high.astype(F32)).astype(jnp.bfloat16)
    return jnp.dot(jnp.concatenate([high, low], 1), matrix, preferred_element_type=F32)


def add_rows(ref, rows):
    for r, plane in rows:
        ref[:, r, :] = ref[:, r, :] + plane


def interior_kernel(first, *refs):
    refs = list(refs)
    take = lambda n: [refs.pop(0) for _ in range(n)]
    zonal, merid, press = take(3)
    if first:
        vert = take(1)[0]
    else:
        uc, vc = take(2)
    zonal_out, merid_out, part = take(3)
    if first:
        copy = pltpu.make_async_copy(vert, take(1)[0], refs.pop())
        copy.start()
    pe, ue, square = take(3)
    depth, ni, nj = press.shape
    per = nj // ni
    rows = per * ni
    matrix = lane_matrix(nj)
    edge = jnp.zeros((depth, nj), F32)
    for ref in (pe, ue):
        ref[:, PAD - 1, :] = edge
        ref[:, PAD + ni, :] = edge
    above, below = slice(PAD + 1, PAD + 1 + ni), slice(PAD - 1, PAD - 1 + ni)
    if not first:
        square[...] = jnp.zeros(square.shape, F32)
    for b in range(depth // per):
        here = slice(b * per, (b + 1) * per)
        pe[here, PAD : PAD + ni, :] = press[here]
        zonal_out[here] = zonal[here] - H_STEP * (pe[here, above, :] - pe[here, below, :])
    if not first:
        add_rows(zonal_out, ((0, uc[0]), (ni - 1, uc[1])))
    for b in range(depth // per):
        here = slice(b * per, (b + 1) * per)
        p = press[here].reshape(rows, nj)
        ue[here, PAD : PAD + ni, :] = zonal_out[here]
        v = merid[here].reshape(rows, nj)
        if not first:
            square[0:1, :] = vc[0, b : b + 1, :]
            square[nj - 1 : nj, :] = vc[1, b : b + 1, :]
            v = v + square[...].T
        v = v - H_STEP * lane_difference(p, matrix)
        merid_out[here] = v.reshape(per, ni, nj)
        spread = (ue[here, above, :] - ue[here, below, :]).reshape(rows, nj) + lane_difference(v, matrix)
        part[here] = (p - D_STEP * spread).reshape(per, ni, nj)
    if first:
        copy.wait()


def emit_kernel(zonal, merid, uc, vc, zonal_out, merid_out, square):
    depth, ni, nj = zonal.shape
    per = nj // ni
    square[...] = jnp.zeros(square.shape, F32)
    for b in range(depth // per):
        here = slice(b * per, (b + 1) * per)
        square[0:1, :] = vc[0, b : b + 1, :]
        square[nj - 1 : nj, :] = vc[1, b : b + 1, :]
        merid_out[here] = merid[here] + square[...].T.reshape(per, ni, nj)
        zonal_out[here] = zonal[here]
    add_rows(zonal_out, ((0, uc[0]), (ni - 1, uc[1])))


def solve_kernel(first, final, hx, hy, groups, *refs):
    refs = list(refs)
    take = lambda n: [refs.pop(0) for _ in range(n)]
    paired = groups == 4
    part0, vert, inv, mul = take(4)
    ox, oy = take(hx.count), take(hy.count)
    rx, ry = take(hx.count), take(hy.count)
    uh, vh = (None, None) if first else take(2)
    if paired:
        own_s, mate_s = take(2) if first else (None, None)
        cf = None if first else take(1)[0]
    y_out, part, planes, uc, vc = take(5)
    across = take(2) if paired else None
    if paired and first:
        cf = take(1)[0]
    uh_out, vh_out = (None, None) if final else take(2)
    square = take(1)[0]
    depth, ni, nj = part0.shape
    last, half, per = depth - 1, depth // 2, nj // ni
    group = lax.axis_index("lev")
    even_x, even_y = lax.axis_index("gx") % 2 == 0, lax.axis_index("gy") % 2 == 0
    if paired and first:
        condense(group, own_s, mate_s, cf)

    u_lo = hx.low(rx, 2, even_x) if first else uh[0]
    u_hi = hx.high(rx, 2, even_x) if first else uh[1]
    u_lo = u_lo - H_STEP * (hx.down(ox, 0, even_x) - hx.low(rx, 0, even_x))
    u_hi = u_hi - H_STEP * (hx.high(rx, 1, even_x) - hx.up(ox, 1, even_x))
    u_first, u_last = H_STEP * hx.low(rx, 1, even_x), -H_STEP * hx.high(rx, 0, even_x)
    uc[0], uc[1] = u_first, u_last
    v_lo = hy.low(ry, 2, even_y) if first else vh[0]
    v_hi = hy.high(ry, 2, even_y) if first else vh[1]
    v_lo = v_lo - H_STEP * (hy.down(oy, 0, even_y) - hy.low(ry, 0, even_y))
    v_hi = v_hi - H_STEP * (hy.high(ry, 1, even_y) - hy.up(oy, 1, even_y))
    if not final:
        uh_out[0], uh_out[1] = u_lo, u_hi
        vh_out[0], vh_out[1] = v_lo, v_hi
    v_first, v_last = H_STEP * hy.low(ry, 1, even_y), -H_STEP * hy.high(ry, 0, even_y)
    vc[0], vc[1] = v_first, v_last
    square[...] = jnp.zeros(square.shape, F32)
    for b in range(depth // per):
        here = slice(b * per, (b + 1) * per)
        one = slice(b, b + 1)
        square[0:1, :] = D_STEP * v_lo[one]
        square[1:2, :] = D_STEP * v_first[one]
        square[nj - 2 : nj - 1, :] = -D_STEP * v_last[one]
        square[nj - 1 : nj, :] = -D_STEP * v_hi[one]
        part[here] = part0[here] + square[...].T.reshape(per, ni, nj)
    edges = ((0, D_STEP * u_lo), (1, D_STEP * u_first), (ni - 2, -D_STEP * u_last), (ni - 1, -D_STEP * u_hi))
    add_rows(part, edges)

    lo = vert[0] - V_STEP * part[1]
    hi = vert[last] + V_STEP * part[last - 1]
    y_out[0], y_out[last] = lo, hi
    for s in range(1, half):
        k, j = s, last - s
        lo = (vert[k] - V_STEP * (part[k + 1] - part[k - 1])) + mul[k] * lo
        hi = (vert[j] - V_STEP * (part[j + 1] - part[j - 1])) + mul[j + 1] * hi
        y_out[k], y_out[j] = lo, hi
    hi = inv[half] * (hi + mul[half] * lo)
    lo = inv[half - 1] * lo + mul[half] * hi
    y_out[half], y_out[half - 1] = hi, lo
    for s in range(1, half):
        k, j = half - 1 - s, half + s
        lo = inv[k] * y_out[k] + mul[k + 1] * lo
        hi = inv[j] * y_out[j] + mul[j] * hi
        y_out[k], y_out[j] = lo, hi
    p_first, p_last = part[0], part[last]
    planes[0], planes[1] = lo, hi
    planes[2], planes[3] = p_first, p_last
    if paired:
        lower = group < 2
        sign = jnp.where(lower, V_STEP, -V_STEP)
        y_near, y_far = jnp.where(lower, hi, lo), jnp.where(lower, lo, hi)
        p_near, p_far = jnp.where(lower, p_last, p_first), jnp.where(lower, p_first, p_last)
        gain = cf[4] * cf[0]
        inside = y_near - gain * (cf[5] * (sign * p_far) + y_far)
        outside = cf[4] * (sign * p_near) + gain * (y_near - cf[6] * (sign * p_near))
        inside = jnp.where((group == 1) | (group == 2), inside, outside)
        for message in across:
            message[0], message[1] = inside, p_near
        if first:
            across[0][2], across[0][3] = cf[1], cf[7]


def paired_sources(group, cf, own, mate, crossed, lv):
    lower = group < 2
    is_inner = (group == 1) | (group == 2)
    sign = jnp.where(lower, V_STEP, -V_STEP)
    near = jnp.where(lower, 1, 0)
    slot = jnp.where(is_inner, 0, 1)
    lv[slot] = own[...]
    lv[1 - slot] = mate[...]
    kappa, mine, other, gain, x, g_out, g_in = (cf[n] for n in range(7))
    y_in_near, y_in_far, y_out = lv[0, near], lv[0, 1 - near], lv[1, near]
    p_in_near = sign * lv[0, 2 + near]
    p_in_far = sign * lv[0, 3 - near]
    p_out = sign * lv[1, 2 + near]
    flux = kappa * ((y_out - g_out * p_in_far) - (y_in_far + g_in * p_out))
    here = y_in_near + x * (p_out + flux)
    there = crossed[0][0] + crossed[1][0]
    p_there = sign * jnp.where(is_inner, crossed[1][1], crossed[0][1])
    middle = gain * ((there - here) + (other * p_in_near + mine * p_there))
    n_here = middle - p_there
    n_there = p_in_near - middle
    flux = flux - kappa * x * n_here
    in_far = p_out + flux
    out_near = -(p_in_far + flux)
    near_source = jnp.where(is_inner, n_here, out_near)
    far_source = jnp.where(is_inner, in_far, 0.0)
    alpha = jnp.where(lower, far_source, near_source)
    beta = jnp.where(lower, near_source, far_source)
    under = jnp.where(
        group == 1,
        y_out + g_out * out_near,
        jnp.where(
            group == 2,
            there + other * n_there,
            jnp.where(group == 3, y_in_far + g_in * in_far + x * n_here, 0.0),
        ),
    )
    return alpha, beta, under


def chain_sources(groups, group, st, own, got, lv):
    lv[group] = own[...]
    for m in range(1, groups):
        lv[source_of(group, m, groups)] = got[m - 1][...]
    zero = jnp.zeros(own.shape[1:], F32)
    z_top, z_bot = [], []
    for g in range(groups):
        below = V_STEP * lv[g - 1, 3] if g else zero
        above = V_STEP * lv[g + 1, 2] if g < groups - 1 else zero
        z_top.append(lv[g, 0] + st[g, 0] * below - st[g, 1] * above)
        z_bot.append(lv[g, 1] + st[g, 1] * below - st[g, 2] * above)
    ratios, parts = [zero], [zero]
    for g in range(1, groups):
        cg = st[g, 3]
        down = cg * st[g - 1, 1]
        pivot = 1.0 / (1.0 + cg * (st[g - 1, 2] + st[g, 0]) - down * ratios[-1])
        parts.append((cg * (z_bot[g - 1] - z_top[g]) + down * parts[-1]) * pivot)
        ratios.append(cg * st[g, 1] * pivot)
    flux = [zero] * (groups + 1)
    for g in range(groups - 1, 0, -1):
        flux[g] = parts[g] + ratios[g] * flux[g + 1]
    alpha, beta, under = zero, zero, zero
    for g in range(groups):
        mine = group == g
        if g:
            alpha = jnp.where(mine, V_STEP * lv[g - 1, 3] + flux[g], alpha)
            bot = z_bot[g - 1] + st[g - 1, 1] * flux[g - 1] - st[g - 1, 2] * flux[g]
            under = jnp.where(mine, bot, under)
        if g < groups - 1:
            beta = jnp.where(mine, -(V_STEP * lv[g + 1, 2] + flux[g + 1]), beta)
    return alpha, beta, under


def finish_kernel(groups, first, final, hx, hy, *refs):
    refs = list(refs)
    take = lambda n: [refs.pop(0) for _ in range(n)]
    y, part, g0, gl, own = take(5)
    got = take(groups - 1)
    paired = groups == 4
    system = take(1)[0]
    setups = take(groups) if first and not paired else ()
    vert_out, press_out = take(2)
    mx, my = ([], []) if final else (take(hx.count), take(hy.count))
    if first:
        early, system = system, take(1)[0]
    lv = take(1)[0]
    depth, _, _ = y.shape
    group = lax.axis_index("lev")
    if paired:
        if first:
            for n in (0, 1, 4, 5, 6):
                system[n] = early[n]
            other = got[1][2]
            c = jnp.where(group < 2, got[1][3], early[7])
            system[2] = other
            system[3] = c / (1.0 + c * (early[1] + other))
        alpha, beta, under = paired_sources(group, system, own, got[0], got[1:], lv)
    else:
        if first:
            spread_setup(groups, group, setups[0], setups[1:], system)
        alpha, beta, under = chain_sources(groups, group, system, own, got, lv)
    vert, press = take(2) if final else (vert_out, press_out)

    def level(k, w_prev):
        w = y[k] + g0[k] * alpha + gl[k] * beta
        vert[k] = w
        press[k] = part[k] - P_STEP * (w - w_prev)
        return w

    if final:
        sems = take(1)[0]
        step, w, copies = max(depth // 4, 1), under, []
        for start in range(0, depth, step):
            stop = min(start + step, depth)
            w = lax.fori_loop(start, stop, level, w, unroll=True)
            for n, (a, b) in enumerate(((vert, vert_out), (press, press_out))):
                here = pl.ds(start, stop - start)
                copies.append(pltpu.make_async_copy(a.at[here], b.at[here], sems.at[n, start // step]))
                copies[-1].start()
        for copy in copies:
            copy.wait()
        return
    lax.fori_loop(0, depth, level, under, unroll=4)
    both_x, both_y = take(2)
    pack_pressure(press_out, both_x, both_y)
    hx.write(mx, both_x, lax.axis_index("gx") % 2 == 0)
    hy.write(my, both_y, lax.axis_index("gy") % 2 == 0)


def body(zonal, meridional, vertical, pressure, coupling, surface, lid_flag):
    depth, ni, nj = coupling.shape
    full, four, two = (depth, ni, nj), (4, ni, nj), (2, ni, nj)
    groups = lax.axis_size("lev")
    hx = Halo("gx", (depth, nj))
    hy = Halo("gy", (depth // (nj // ni), nj))
    wide = pltpu.VMEM((depth, ni + 2 * PAD, nj), F32)
    square = pltpu.VMEM((nj, nj), F32)

    inputs = (pressure, meridional, zonal, coupling, surface, lid_flag)
    results = call(
        functools.partial(first_kernel, hx, hy),
        [full] * 4 + [surface.shape] * 2 + hx.shapes(3) + hy.shapes(3),
        [pltpu.with_memory_space_constraint(a, pltpu.HBM) for a in inputs],
        scratch=[hx.scratch(3), hy.scratch(3), pltpu.SemaphoreType.DMA((6,))],
        spaces=[HBM] * 6,
        types=[a.dtype for a in inputs],
    )
    pressure, meridional, zonal, coupling, surface, lid_flag = results[:6]
    ox, oy = results[6 : 6 + hx.count], results[6 + hx.count :]
    ry, rx = hy.exchange(oy), hx.exchange(ox)
    inv, mul, g0, gl, own_s = call(
        functools.partial(factor_kernel, groups), [full] * 4 + [four], [coupling, surface, lid_flag]
    )
    paired = groups == 4
    got_s = [to_lev(own_s, m) for m in range(1, 2 if paired else groups)]
    setup = (8 if paired else 4 * groups, ni, nj)
    system = uh = vh = uc = vc = None
    for substep in range(SUBSTEPS):
        first, final = substep == 0, substep == SUBSTEPS - 1
        args = [zonal, meridional, pressure]
        args += [pltpu.with_memory_space_constraint(vertical, pltpu.HBM)] if first else [uc, vc]
        results = call(
            functools.partial(interior_kernel, first),
            [full] * (4 if first else 3),
            args,
            scratch=[wide, wide, square] + ([pltpu.SemaphoreType.DMA(())] if first else []),
            spaces=[VMEM] * 3 + [HBM] if first else None,
        )
        zonal, meridional, part = results[:3]
        if first:
            vertical = results[3]
        args = [part, vertical, inv, mul] + ox + oy + rx + ry
        args += [] if first else [uh, vh]
        if paired:
            args += [own_s] + got_s if first else [system]
        ends = [(2,) + hx.plane, (2,) + hy.plane]
        outs = [full, full, four] + ends
        if paired:
            outs += [four if first else two, two] + ([setup] if first else [])
        outs += [] if final else ends
        results = call(functools.partial(solve_kernel, first, final, hx, hy, groups), outs, args, scratch=[square])
        y, part, own, uc, vc = results[:5]
        if not final:
            uh, vh = results[-2:]
        if paired:
            got = [to_lev(a, m) for m, a in ((1, own), (2, results[5]), (3, results[6]))]
            if first:
                system = results[7]
        else:
            got = [to_lev(own, m) for m in range(1, groups)]
        if final:
            zonal, meridional = call(emit_kernel, [full] * 2, [zonal, meridional, uc, vc], scratch=[square])
        args = [y, part, g0, gl, own] + got + [own_s if system is None else system]
        if first and not paired:
            args += [own_s] + got_s
        outs, scratch = [full, full], [pltpu.VMEM((groups, 4, ni, nj), F32)]
        if not final:
            outs += hx.shapes(2) + hy.shapes(2)
        if first:
            outs += [setup if paired else (groups, 4, ni, nj)]
        if final:
            scratch += [pltpu.VMEM(full, F32)] * 2 + [pltpu.SemaphoreType.DMA((2, 4))]
        else:
            scratch += [hx.scratch(2), hy.scratch(2)]
        results = call(
            functools.partial(finish_kernel, groups, first, final, hx, hy),
            outs,
            args,
            scratch=scratch,
            out_spaces=[HBM] * 2 if final else None,
        )
        vertical, pressure = results[:2]
        if first:
            system = results[-1]
        if not final:
            ox, oy = results[2 : 2 + hx.count], results[2 + hx.count : 2 + hx.count + hy.count]
            ry, rx = hy.exchange(oy), hx.exchange(ox)
    return (zonal, meridional, vertical, pressure)


def solution(mesh):
    block = P("lev", "gx", "gy")
    plane = P("gx", "gy")

    return jax.shard_map(
        body,
        mesh=mesh,
        in_specs=(block,) * 5 + (plane,) * 2,
        out_specs=(block,) * 4,
        check_vma=False,
    )
```

```python
import functools

import jax
import jax.numpy as jnp
from jax import lax
from jax.experimental import pallas as pl
from jax.experimental.pallas import tpu as pltpu
from jax.sharding import PartitionSpec as P

SUBSTEPS = 3
H_STEP = 0.25
D_STEP = 0.25
V_STEP = 0.5
P_STEP = 0.5
F32 = jnp.float32
PAD = 8

VMEM = pl.BlockSpec(memory_space=pltpu.VMEM)
HBM = pl.BlockSpec(memory_space=pltpu.HBM)


def call(kernel, outs, args, scratch=(), spaces=None, out_spaces=None, types=()):
    return list(
        pl.pallas_call(
            kernel,
            out_shape=[jax.ShapeDtypeStruct(s, types[n] if n < len(types) else F32) for n, s in enumerate(outs)],
            in_specs=spaces or [VMEM] * len(args),
            out_specs=out_spaces or [VMEM] * len(outs),
            scratch_shapes=list(scratch),
            compiler_params=pltpu.CompilerParams(vmem_limit_bytes=20 * 1024 * 1024),
        )(*args)
    )


class Halo:
    def __init__(self, axis, plane):
        self.axis, self.plane = axis, plane
        self.n = lax.axis_size(axis)
        self.count = 1 if self.n <= 2 else 2
        self.swap = self.n > 2 and self.n % 2 == 0

    def shapes(self, rows):
        return [(2 * rows,) + self.plane] if self.count == 1 else [(rows,) + self.plane] * 2

    def scratch(self, rows):
        return pltpu.VMEM((2, rows) + self.plane, F32)

    def write(self, refs, both, even):
        rows = both.shape[1]
        if self.count == 1:
            refs[0][:rows] = both[0]
            refs[0][rows:] = both[1]
        elif self.swap:
            refs[0][...] = jnp.where(even, both[0], both[1])
            refs[1][...] = jnp.where(even, both[1], both[0])
        else:
            refs[0][...] = both[0]
            refs[1][...] = both[1]

    def up(self, refs, r, even):
        if self.swap:
            return jnp.where(even, refs[0][r], refs[1][r])
        return refs[0][r]

    def down(self, refs, r, even):
        if self.swap:
            return jnp.where(even, refs[1][r], refs[0][r])
        return refs[0][refs[0].shape[0] // 2 + r] if self.count == 1 else refs[1][r]

    def low(self, refs, r, even):
        if self.swap:
            return jnp.where(even, refs[1][r], refs[0][r])
        return refs[0][r]

    def high(self, refs, r, even):
        if self.swap:
            return jnp.where(even, refs[0][r], refs[1][r])
        return refs[0][refs[0].shape[0] // 2 + r] if self.count == 1 else refs[1][r]

    def exchange(self, messages):
        n = self.n
        if n == 1:
            return messages
        if self.swap:
            first = [(i, i ^ 1) for i in range(n)]
            second = [(i, (i + 1) % n if i % 2 else (i - 1) % n) for i in range(n)]
            got = lax.ppermute(messages[1], self.axis, second)
            return [lax.ppermute(messages[0], self.axis, first), got]
        up = [(i, (i + 1) % n) for i in range(n)]
        if n == 2:
            return [lax.ppermute(messages[0], self.axis, up)]
        down = [(j, i) for i, j in up]
        return [lax.ppermute(messages[0], self.axis, up), lax.ppermute(messages[1], self.axis, down)]


def to_lev(message, m):
    n = lax.axis_size("lev")
    if n & (n - 1) == 0:
        return lax.ppermute(message, "lev", [(i, i ^ m) for i in range(n)])
    return lax.ppermute(message, "lev", [(i, (i + m) % n) for i in range(n)])


def source_of(group, m, n):
    return group ^ m if n & (n - 1) == 0 else (group - m) % n


def pack_columns(ref, picks, outs, b):
    ni, nj = ref.shape[1:]
    per = nj // ni
    turned = ref[b * per : (b + 1) * per].reshape(per * ni, nj).T
    for c, out in zip(picks, outs):
        out[b : b + 1, :] = turned[c : c + 1, :]


def pack_pressure(press, both_x, both_y, b):
    ni, nj = press.shape[1:]
    per = nj // ni
    here = slice(b * per, (b + 1) * per)
    for r in range(2):
        both_x[0, r, here] = press[here, ni - 2 + r, :]
        both_x[1, r, here] = press[here, r, :]
    outs = (both_y.at[0, 0], both_y.at[0, 1], both_y.at[1, 0], both_y.at[1, 1])
    pack_columns(press, (nj - 2, nj - 1, 0, 1), outs, b)


def first_kernel(hx, hy, *refs):
    refs = list(refs)
    take = lambda n: [refs.pop(0) for _ in range(n)]
    sources, targets = take(3), take(3)
    mx, my = take(hx.count), take(hy.count)
    both_x, both_y, sems = refs
    p, v, u = targets[:3]
    copies = [pltpu.make_async_copy(a, b, sems.at[n]) for n, (a, b) in enumerate(zip(sources, targets))]
    for copy in copies:
        copy.start()
    ni, nj = p.shape[1:]
    blocks = range(p.shape[0] // (nj // ni))
    copies[0].wait()
    for b in blocks:
        pack_pressure(p, both_x, both_y, b)
    copies[1].wait()
    for b in blocks:
        pack_columns(v, (nj - 1, 0), (both_y.at[0, 2], both_y.at[1, 2]), b)
    copies[2].wait()
    both_x[0, 2] = u[:, ni - 1, :]
    both_x[1, 2] = u[:, 0, :]
    hx.write(mx, both_x, lax.axis_index("gx") % 2 == 0)
    hy.write(my, both_y, lax.axis_index("gy") % 2 == 0)
    for copy in copies[3:]:
        copy.wait()


def factor_kernel(groups, c, surface, lid, inv, mul, g0, gl, planes):
    depth, ni, nj = c.shape
    last, half = depth - 1, depth // 2
    group = lax.axis_index("lev")
    bottom = group == 0
    top = group == groups - 1
    ground = surface[...] - group * depth
    lidf = jnp.where(top, lid[...].astype(F32), 0.0)

    def coupling(k):
        return jnp.where(ground <= k - 1, c[k], 0.0)

    def diag(k):
        low = c[k] if k > 0 else jnp.where(bottom, c[k], 0.0)
        high = c[k + 1] if k < last else lidf * c[k]
        return 1.0 + low + high

    lo, hi = None, None
    for s in range(half):
        k, j = s, last - s
        d_lo, d_hi = diag(k), diag(j)
        if s:
            e_lo = coupling(k)
            m_lo = e_lo * lo
            mul[k] = m_lo
            d_lo = d_lo - e_lo * m_lo
            e_hi = coupling(j + 1)
            m_hi = e_hi * hi
            mul[j + 1] = m_hi
            d_hi = d_hi - e_hi * m_hi
        if j == half:
            e_mid = coupling(half)
            lo = jnp.where(ground <= k, 1.0 / d_lo, 0.0)
            m_mid = e_mid * lo
            mul[half] = m_mid
            d_hi = d_hi - e_mid * m_mid
        else:
            lo = jnp.where(ground <= k, 1.0 / d_lo, 0.0)
        hi = jnp.where(ground <= j, 1.0 / d_hi, 0.0)
        inv[k] = lo
        inv[j] = hi
    one = jnp.ones((ni, nj), F32)
    t0 = [one] + [None] * (half - 1)
    tl = [one] + [None] * (half - 1)
    for s in range(1, half):
        t0[s] = mul[s] * t0[s - 1]
        tl[s] = mul[last - s + 1] * tl[s - 1]
        g0[s] = t0[s]
        gl[last - s] = tl[s]
    g0[0] = one
    gl[last] = one
    xh0 = inv[half] * (mul[half] * t0[half - 1])
    xhl = inv[half] * tl[half - 1]
    xk0 = inv[half - 1] * t0[half - 1] + mul[half] * xh0
    xkl = mul[half] * xhl
    g0[half], gl[half] = xh0, xhl
    g0[half - 1], gl[half - 1] = xk0, xkl
    for s in range(1, half):
        k, j = half - 1 - s, half + s
        xk0 = inv[k] * g0[k] + mul[k + 1] * xk0
        xkl = mul[k + 1] * xkl
        xh0 = mul[j] * xh0
        xhl = inv[j] * gl[j] + mul[j] * xhl
        g0[k], gl[k] = xk0, xkl
        g0[j], gl[j] = xh0, xhl
    planes[0] = g0[0]
    planes[1] = g0[last]
    planes[2] = gl[last]
    planes[3] = c[0]


def condense(group, own, mate, cf):
    lower = group < 2
    is_inner = (group == 1) | (group == 2)
    inner = [jnp.where(is_inner, own[n], mate[n]) for n in range(4)]
    outer = [jnp.where(is_inner, mate[n], own[n]) for n in range(4)]
    x = inner[1]
    g_out, g_in = jnp.where(lower, outer[2], outer[0]), jnp.where(lower, inner[0], inner[2])
    c = jnp.where(lower, inner[3], outer[3])
    kappa = c / (1.0 + c * (g_out + g_in))
    cf[0] = kappa
    cf[1] = jnp.where(lower, inner[2], inner[0]) - kappa * x * x
    cf[2] = jnp.zeros_like(x)
    cf[3] = jnp.zeros_like(x)
    cf[4] = x
    cf[5] = g_out
    cf[6] = g_in
    cf[7] = inner[3]


def spread_setup(groups, group, own, got, st):
    st[group] = own[...]
    for m in range(1, groups):
        st[source_of(group, m, groups)] = got[m - 1][...]


def lane_matrix(nj):
    src = lax.broadcasted_iota(jnp.int32, (2 * nj, nj), 0) % nj
    dst = lax.broadcasted_iota(jnp.int32, (2 * nj, nj), 1)
    return jnp.where(src == dst + 1, 1.0, jnp.where(src == dst - 1, -1.0, 0.0)).astype(jnp.bfloat16)


def lane_difference(x, matrix):
    high = x.astype(jnp.bfloat16)
    low = (x - high.astype(F32)).astype(jnp.bfloat16)
    return jnp.dot(jnp.concatenate([high, low], 1), matrix, preferred_element_type=F32)


def at_lanes(low, high, nj):
    tile = 8
    place = lax.broadcasted_iota(jnp.int32, (tile, nj), 0)
    top = bottom = jnp.zeros((tile, nj), F32)
    for n, row in enumerate(low):
        top = jnp.where(place == n, row, top)
    for n, row in enumerate(high):
        bottom = jnp.where(place == tile - len(high) + n, row, bottom)
    return jnp.concatenate([top, jnp.zeros((nj - 2 * tile, nj), F32), bottom], 0).T


def add_rows(ref, rows):
    for r, plane in rows:
        ref[:, r, :] = ref[:, r, :] + plane


def interior_kernel(first, *refs):
    refs = list(refs)
    take = lambda n: [refs.pop(0) for _ in range(n)]
    zonal, merid, press = take(3)
    uc, vc = (None, None) if first else take(2)
    zonal_out, merid_out, part = take(3)
    pe, ue = take(2)
    depth, ni, nj = press.shape
    per = nj // ni
    rows = per * ni
    matrix = lane_matrix(nj)
    edge = jnp.zeros((depth, nj), F32)
    for ref in (pe, ue):
        ref[:, PAD - 1, :] = edge
        ref[:, PAD + ni, :] = edge
    above, below = slice(PAD + 1, PAD + 1 + ni), slice(PAD - 1, PAD - 1 + ni)
    for b in range(depth // per):
        here = slice(b * per, (b + 1) * per)
        pe[here, PAD : PAD + ni, :] = press[here]
        zonal_out[here] = zonal[here] - H_STEP * (pe[here, above, :] - pe[here, below, :])
    if not first:
        add_rows(zonal_out, ((0, uc[0]), (ni - 1, uc[1])))
    for b in range(depth // per):
        here = slice(b * per, (b + 1) * per)
        p = press[here].reshape(rows, nj)
        ue[here, PAD : PAD + ni, :] = zonal_out[here]
        v = merid[here].reshape(rows, nj)
        if not first:
            v = v + at_lanes((vc[0, b : b + 1, :],), (vc[1, b : b + 1, :],), nj)
        v = v - H_STEP * lane_difference(p, matrix)
        merid_out[here] = v.reshape(per, ni, nj)
        spread = (ue[here, above, :] - ue[here, below, :]).reshape(rows, nj) + lane_difference(v, matrix)
        part[here] = (p - D_STEP * spread).reshape(per, ni, nj)


def emit_kernel(zonal, merid, uc, vc, zonal_out, merid_out):
    depth, ni, nj = zonal.shape
    per = nj // ni
    for b in range(depth // per):
        here = slice(b * per, (b + 1) * per)
        turned = at_lanes((vc[0, b : b + 1, :],), (vc[1, b : b + 1, :],), nj)
        merid_out[here] = merid[here] + turned.reshape(per, ni, nj)
        zonal_out[here] = zonal[here]
    add_rows(zonal_out, ((0, uc[0]), (ni - 1, uc[1])))


def solve_kernel(first, final, hx, hy, groups, *refs):
    refs = list(refs)
    take = lambda n: [refs.pop(0) for _ in range(n)]
    paired = groups == 4
    part0, vert, inv, mul = take(4)
    ox, oy = take(hx.count), take(hy.count)
    rx, ry = take(hx.count), take(hy.count)
    uh, vh = (None, None) if first else take(2)
    if paired:
        own_s, mate_s = take(2) if first else (None, None)
        cf = None if first else take(1)[0]
    y_out, part, planes, uc, vc = take(5)
    across = take(2) if paired else None
    if paired and first:
        cf = take(1)[0]
    uh_out, vh_out = (None, None) if final else take(2)
    rows = take(1)[0]
    depth, ni, nj = part0.shape
    last, half, per = depth - 1, depth // 2, nj // ni
    group = lax.axis_index("lev")
    even_x, even_y = lax.axis_index("gx") % 2 == 0, lax.axis_index("gy") % 2 == 0
    if paired and first:
        condense(group, own_s, mate_s, cf)

    u_lo = hx.low(rx, 2, even_x) if first else uh[0]
    u_hi = hx.high(rx, 2, even_x) if first else uh[1]
    u_lo = u_lo - H_STEP * (hx.down(ox, 0, even_x) - hx.low(rx, 0, even_x))
    u_hi = u_hi - H_STEP * (hx.high(rx, 1, even_x) - hx.up(ox, 1, even_x))
    u_first, u_last = H_STEP * hx.low(rx, 1, even_x), -H_STEP * hx.high(rx, 0, even_x)
    uc[0], uc[1] = u_first, u_last
    v_lo = hy.low(ry, 2, even_y) if first else vh[0]
    v_hi = hy.high(ry, 2, even_y) if first else vh[1]
    v_lo = v_lo - H_STEP * (hy.down(oy, 0, even_y) - hy.low(ry, 0, even_y))
    v_hi = v_hi - H_STEP * (hy.high(ry, 1, even_y) - hy.up(oy, 1, even_y))
    if not final:
        uh_out[0], uh_out[1] = u_lo, u_hi
        vh_out[0], vh_out[1] = v_lo, v_hi
    v_first, v_last = H_STEP * hy.low(ry, 1, even_y), -H_STEP * hy.high(ry, 0, even_y)
    vc[0], vc[1] = v_first, v_last
    edges = ((0, D_STEP * u_lo), (1, D_STEP * u_first), (ni - 2, -D_STEP * u_last), (ni - 1, -D_STEP * u_hi))
    for n, (_, plane) in enumerate(edges):
        rows[n] = plane
    blocks = depth // per
    for b in [x for pair in zip(range(blocks // 2), range(blocks - 1, -1, -1)) for x in pair] + [blocks // 2] * (blocks % 2):
        here, one = slice(b * per, (b + 1) * per), slice(b, b + 1)
        low = (D_STEP * v_lo[one], D_STEP * v_first[one])
        high = (-D_STEP * v_last[one], -D_STEP * v_hi[one])
        part[here] = part0[here] + at_lanes(low, high, nj).reshape(per, ni, nj)
        for n, (r, _) in enumerate(edges):
            part[here, r, :] = part[here, r, :] + rows[n, here]

    lo = vert[0] - V_STEP * part[1]
    hi = vert[last] + V_STEP * part[last - 1]
    y_out[0], y_out[last] = lo, hi
    for s in range(1, half):
        k, j = s, last - s
        lo = (vert[k] - V_STEP * (part[k + 1] - part[k - 1])) + mul[k] * lo
        hi = (vert[j] - V_STEP * (part[j + 1] - part[j - 1])) + mul[j + 1] * hi
        y_out[k], y_out[j] = lo, hi
    hi = inv[half] * (hi + mul[half] * lo)
    lo = inv[half - 1] * lo + mul[half] * hi
    y_out[half], y_out[half - 1] = hi, lo
    for s in range(1, half):
        k, j = half - 1 - s, half + s
        lo = inv[k] * y_out[k] + mul[k + 1] * lo
        hi = inv[j] * y_out[j] + mul[j] * hi
        y_out[k], y_out[j] = lo, hi
    p_first, p_last = part[0], part[last]
    planes[0], planes[1] = lo, hi
    planes[2], planes[3] = p_first, p_last
    if paired:
        lower = group < 2
        sign = jnp.where(lower, V_STEP, -V_STEP)
        y_near, y_far = jnp.where(lower, hi, lo), jnp.where(lower, lo, hi)
        p_near, p_far = jnp.where(lower, p_last, p_first), jnp.where(lower, p_first, p_last)
        gain = cf[4] * cf[0]
        inside = y_near - gain * (cf[5] * (sign * p_far) + y_far)
        outside = cf[4] * (sign * p_near) + gain * (y_near - cf[6] * (sign * p_near))
        inside = jnp.where((group == 1) | (group == 2), inside, outside)
        for message in across:
            message[0], message[1] = inside, p_near
        if first:
            across[0][2], across[0][3] = cf[1], cf[7]


def paired_sources(group, cf, own, mate, crossed, lv):
    lower = group < 2
    is_inner = (group == 1) | (group == 2)
    sign = jnp.where(lower, V_STEP, -V_STEP)
    near = jnp.where(lower, 1, 0)
    slot = jnp.where(is_inner, 0, 1)
    lv[slot] = own[...]
    lv[1 - slot] = mate[...]
    kappa, mine, other, gain, x, g_out, g_in = (cf[n] for n in range(7))
    y_in_near, y_in_far, y_out = lv[0, near], lv[0, 1 - near], lv[1, near]
    p_in_near = sign * lv[0, 2 + near]
    p_in_far = sign * lv[0, 3 - near]
    p_out = sign * lv[1, 2 + near]
    flux = kappa * ((y_out - g_out * p_in_far) - (y_in_far + g_in * p_out))
    here = y_in_near + x * (p_out + flux)
    there = crossed[0][0] + crossed[1][0]
    p_there = sign * jnp.where(is_inner, crossed[1][1], crossed[0][1])
    middle = gain * ((there - here) + (other * p_in_near + mine * p_there))
    n_here = middle - p_there
    n_there = p_in_near - middle
    flux = flux - kappa * x * n_here
    in_far = p_out + flux
    out_near = -(p_in_far + flux)
    near_source = jnp.where(is_inner, n_here, out_near)
    far_source = jnp.where(is_inner, in_far, 0.0)
    alpha = jnp.where(lower, far_source, near_source)
    beta = jnp.where(lower, near_source, far_source)
    under = jnp.where(
        group == 1,
        y_out + g_out * out_near,
        jnp.where(
            group == 2,
            there + other * n_there,
            jnp.where(group == 3, y_in_far + g_in * in_far + x * n_here, 0.0),
        ),
    )
    return alpha, beta, under


def chain_sources(groups, group, st, own, got, lv):
    lv[group] = own[...]
    for m in range(1, groups):
        lv[source_of(group, m, groups)] = got[m - 1][...]
    zero = jnp.zeros(own.shape[1:], F32)
    z_top, z_bot = [], []
    for g in range(groups):
        below = V_STEP * lv[g - 1, 3] if g else zero
        above = V_STEP * lv[g + 1, 2] if g < groups - 1 else zero
        z_top.append(lv[g, 0] + st[g, 0] * below - st[g, 1] * above)
        z_bot.append(lv[g, 1] + st[g, 1] * below - st[g, 2] * above)
    ratios, parts = [zero], [zero]
    for g in range(1, groups):
        cg = st[g, 3]
        down = cg * st[g - 1, 1]
        pivot = 1.0 / (1.0 + cg * (st[g - 1, 2] + st[g, 0]) - down * ratios[-1])
        parts.append((cg * (z_bot[g - 1] - z_top[g]) + down * parts[-1]) * pivot)
        ratios.append(cg * st[g, 1] * pivot)
    flux = [zero] * (groups + 1)
    for g in range(groups - 1, 0, -1):
        flux[g] = parts[g] + ratios[g] * flux[g + 1]
    alpha, beta, under = zero, zero, zero
    for g in range(groups):
        mine = group == g
        if g:
            alpha = jnp.where(mine, V_STEP * lv[g - 1, 3] + flux[g], alpha)
            bot = z_bot[g - 1] + st[g - 1, 1] * flux[g - 1] - st[g - 1, 2] * flux[g]
            under = jnp.where(mine, bot, under)
        if g < groups - 1:
            beta = jnp.where(mine, -(V_STEP * lv[g + 1, 2] + flux[g + 1]), beta)
    return alpha, beta, under


def finish_kernel(groups, first, final, hx, hy, *refs):
    refs = list(refs)
    take = lambda n: [refs.pop(0) for _ in range(n)]
    y, part, g0, gl, own = take(5)
    got = take(groups - 1)
    paired = groups == 4
    system = take(1)[0]
    setups = take(groups) if first and not paired else ()
    vert_out, press_out = take(2)
    mx, my = ([], []) if final else (take(hx.count), take(hy.count))
    if first:
        early, system = system, take(1)[0]
    lv = take(1)[0]
    depth, ni, nj = y.shape
    group = lax.axis_index("lev")
    if paired:
        if first:
            for n in (0, 1, 4, 5, 6):
                system[n] = early[n]
            other = got[1][2]
            c = jnp.where(group < 2, got[1][3], early[7])
            system[2] = other
            system[3] = c / (1.0 + c * (early[1] + other))
        alpha, beta, under = paired_sources(group, system, own, got[0], got[1:], lv)
    else:
        if first:
            spread_setup(groups, group, setups[0], setups[1:], system)
        alpha, beta, under = chain_sources(groups, group, system, own, got, lv)
    vert, press = take(2) if final else (vert_out, press_out)

    def level(k, w_prev):
        w = y[k] + g0[k] * alpha + gl[k] * beta
        vert[k] = w
        press[k] = part[k] - P_STEP * (w - w_prev)
        return w

    if final:
        sems = take(1)[0]
        step, w, copies = max(depth // 4, 1), under, []
        for start in range(0, depth, step):
            stop = min(start + step, depth)
            w = lax.fori_loop(start, stop, level, w, unroll=True)
            for n, (a, b) in enumerate(((vert, vert_out), (press, press_out))):
                here = pl.ds(start, stop - start)
                copies.append(pltpu.make_async_copy(a.at[here], b.at[here], sems.at[n, start // step]))
                copies[-1].start()
        for copy in copies:
            copy.wait()
        return
    both_x, both_y = take(2)
    w, per = under, nj // ni
    for k in range(depth):
        w = level(k, w)
        if (k + 1) % per == 0:
            pack_pressure(press_out, both_x, both_y, k // per)
    hx.write(mx, both_x, lax.axis_index("gx") % 2 == 0)
    hy.write(my, both_y, lax.axis_index("gy") % 2 == 0)


def body(zonal, meridional, vertical, pressure, coupling, surface, lid_flag):
    depth, ni, nj = coupling.shape
    full, four, two = (depth, ni, nj), (4, ni, nj), (2, ni, nj)
    groups = lax.axis_size("lev")
    hx = Halo("gx", (depth, nj))
    hy = Halo("gy", (depth // (nj // ni), nj))
    wide = pltpu.VMEM((depth, ni + 2 * PAD, nj), F32)

    inputs = (pressure, meridional, zonal)
    results = call(
        functools.partial(first_kernel, hx, hy),
        [full] * 3 + hx.shapes(3) + hy.shapes(3),
        [pltpu.with_memory_space_constraint(a, pltpu.HBM) for a in inputs],
        scratch=[hx.scratch(3), hy.scratch(3), pltpu.SemaphoreType.DMA((3,))],
        spaces=[HBM] * 3,
        types=[a.dtype for a in inputs],
    )
    pressure, meridional, zonal = results[:3]
    ox, oy = results[3 : 3 + hx.count], results[3 + hx.count :]
    ry, rx = hy.exchange(oy), hx.exchange(ox)
    inv, mul, g0, gl, own_s = call(
        functools.partial(factor_kernel, groups), [full] * 4 + [four], [coupling, surface, lid_flag]
    )
    paired = groups == 4
    got_s = [to_lev(own_s, m) for m in range(1, 2 if paired else groups)]
    setup = (8 if paired else 4 * groups, ni, nj)
    system = uh = vh = uc = vc = None
    for substep in range(SUBSTEPS):
        first, final = substep == 0, substep == SUBSTEPS - 1
        args = [zonal, meridional, pressure]
        args += [] if first else [uc, vc]
        zonal, meridional, part = call(
            functools.partial(interior_kernel, first), [full] * 3, args, scratch=[wide, wide]
        )
        args = [part, vertical, inv, mul] + ox + oy + rx + ry
        args += [] if first else [uh, vh]
        if paired:
            args += [own_s] + got_s if first else [system]
        ends = [(2,) + hx.plane, (2,) + hy.plane]
        outs = [full, full, four] + ends
        if paired:
            outs += [four if first else two, two] + ([setup] if first else [])
        outs += [] if final else ends
        results = call(functools.partial(solve_kernel, first, final, hx, hy, groups), outs, args, scratch=[pltpu.VMEM((4,) + hx.plane, F32)])
        y, part, own, uc, vc = results[:5]
        if not final:
            uh, vh = results[-2:]
        if paired:
            got = [to_lev(a, m) for m, a in ((1, own), (2, results[5]), (3, results[6]))]
            if first:
                system = results[7]
        else:
            got = [to_lev(own, m) for m in range(1, groups)]
        if final:
            zonal, meridional = call(emit_kernel, [full] * 2, [zonal, meridional, uc, vc])
        args = [y, part, g0, gl, own] + got + [own_s if system is None else system]
        if first and not paired:
            args += [own_s] + got_s
        outs, scratch = [full, full], [pltpu.VMEM((groups, 4, ni, nj), F32)]
        if not final:
            outs += hx.shapes(2) + hy.shapes(2)
        if first:
            outs += [setup if paired else (groups, 4, ni, nj)]
        if final:
            scratch += [pltpu.VMEM(full, F32)] * 2 + [pltpu.SemaphoreType.DMA((2, 4))]
        else:
            scratch += [hx.scratch(2), hy.scratch(2)]
        results = call(
            functools.partial(finish_kernel, groups, first, final, hx, hy),
            outs,
            args,
            scratch=scratch,
            out_spaces=[HBM] * 2 if final else None,
        )
        vertical, pressure = results[:2]
        if first:
            system = results[-1]
        if not final:
            ox, oy = results[2 : 2 + hx.count], results[2 + hx.count : 2 + hx.count + hy.count]
            ry, rx = hy.exchange(oy), hx.exchange(ox)
    return (zonal, meridional, vertical, pressure)


def solution(mesh):
    block = P("lev", "gx", "gy")
    plane = P("gx", "gy")

    return jax.shard_map(
        body,
        mesh=mesh,
        in_specs=(block,) * 5 + (plane,) * 2,
        out_specs=(block,) * 4,
        check_vma=False,
    )
```

```python
import functools

import jax
import jax.numpy as jnp
from jax import lax
from jax.experimental import pallas as pl
from jax.experimental.pallas import tpu as pltpu
from jax.sharding import PartitionSpec as P

SUBSTEPS = 3
H_STEP = 0.25
D_STEP = 0.25
V_STEP = 0.5
P_STEP = 0.5
F32 = jnp.float32
PAD = 8

VMEM = pl.BlockSpec(memory_space=pltpu.VMEM)
HBM = pl.BlockSpec(memory_space=pltpu.HBM)


def call(kernel, outs, args, scratch=(), spaces=None, out_spaces=None, types=()):
    return list(
        pl.pallas_call(
            kernel,
            out_shape=[jax.ShapeDtypeStruct(s, types[n] if n < len(types) else F32) for n, s in enumerate(outs)],
            in_specs=spaces or [VMEM] * len(args),
            out_specs=out_spaces or [VMEM] * len(outs),
            scratch_shapes=list(scratch),
            compiler_params=pltpu.CompilerParams(vmem_limit_bytes=20 * 1024 * 1024),
        )(*args)
    )


class Halo:
    def __init__(self, axis, plane):
        self.axis, self.plane = axis, plane
        self.n = lax.axis_size(axis)
        self.count = 1 if self.n <= 2 else 2

    def shapes(self, rows):
        return [(2 * rows,) + self.plane] if self.count == 1 else [(rows,) + self.plane] * 2

    def scratch(self, rows):
        return pltpu.VMEM((2, rows) + self.plane, F32)

    def write(self, refs, both):
        rows = both.shape[1]
        if self.count == 1:
            refs[0][:rows] = both[0]
            refs[0][rows:] = both[1]
        else:
            refs[0][...] = both[0]
            refs[1][...] = both[1]

    def up(self, refs, r):
        return refs[0][r]

    def down(self, refs, r):
        return refs[0][refs[0].shape[0] // 2 + r] if self.count == 1 else refs[1][r]

    def low(self, refs, r):
        return refs[0][r]

    def high(self, refs, r):
        return refs[0][refs[0].shape[0] // 2 + r] if self.count == 1 else refs[1][r]

    def exchange(self, messages):
        n = self.n
        if n == 1:
            return messages
        up = [(i, (i + 1) % n) for i in range(n)]
        if n == 2:
            return [lax.ppermute(messages[0], self.axis, up)]
        down = [(j, i) for i, j in up]
        got = lax.ppermute(messages[0], self.axis, up)
        return [got, lax.ppermute(messages[1], self.axis, down)]


def to_lev(message, m):
    n = lax.axis_size("lev")
    if n & (n - 1) == 0:
        return lax.ppermute(message, "lev", [(i, i ^ m) for i in range(n)])
    return lax.ppermute(message, "lev", [(i, (i + m) % n) for i in range(n)])


def source_of(group, m, n):
    return group ^ m if n & (n - 1) == 0 else (group - m) % n


def pack_columns(ref, picks, outs, b):
    ni, nj = ref.shape[1:]
    per = nj // ni
    turned = ref[b * per : (b + 1) * per].reshape(per * ni, nj).T
    for c, out in zip(picks, outs):
        out[b : b + 1, :] = turned[c : c + 1, :]


def pack_pressure(press, both_x, both_y, b):
    ni, nj = press.shape[1:]
    per = nj // ni
    here = slice(b * per, (b + 1) * per)
    for r in range(2):
        both_x[0, r, here] = press[here, ni - 2 + r, :]
        both_x[1, r, here] = press[here, r, :]
    outs = (both_y.at[0, 0], both_y.at[0, 1], both_y.at[1, 0], both_y.at[1, 1])
    pack_columns(press, (nj - 2, nj - 1, 0, 1), outs, b)


def first_kernel(hx, hy, *refs):
    refs = list(refs)
    take = lambda n: [refs.pop(0) for _ in range(n)]
    sources, targets = take(3), take(3)
    mx, my = take(hx.count), take(hy.count)
    both_x, both_y, sems = refs
    p, v, u = targets[:3]
    copies = [pltpu.make_async_copy(a, b, sems.at[n]) for n, (a, b) in enumerate(zip(sources, targets))]
    for copy in copies:
        copy.start()
    ni, nj = p.shape[1:]
    blocks = range(p.shape[0] // (nj // ni))
    copies[0].wait()
    for b in blocks:
        pack_pressure(p, both_x, both_y, b)
    copies[1].wait()
    for b in blocks:
        pack_columns(v, (nj - 1, 0), (both_y.at[0, 2], both_y.at[1, 2]), b)
    copies[2].wait()
    both_x[0, 2] = u[:, ni - 1, :]
    both_x[1, 2] = u[:, 0, :]
    hx.write(mx, both_x)
    hy.write(my, both_y)
    for copy in copies[3:]:
        copy.wait()


def factor_kernel(groups, c, surface, lid, inv, mul, g0, gl, planes):
    depth, ni, nj = c.shape
    last, half = depth - 1, depth // 2
    group = lax.axis_index("lev")
    bottom = group == 0
    top = group == groups - 1
    ground = surface[...] - group * depth
    lidf = jnp.where(top, lid[...].astype(F32), 0.0)

    def coupling(k):
        return jnp.where(ground <= k - 1, c[k], 0.0)

    def diag(k):
        low = c[k] if k > 0 else jnp.where(bottom, c[k], 0.0)
        high = c[k + 1] if k < last else lidf * c[k]
        return 1.0 + low + high

    lo, hi = None, None
    for s in range(half):
        k, j = s, last - s
        d_lo, d_hi = diag(k), diag(j)
        if s:
            e_lo = coupling(k)
            m_lo = e_lo * lo
            mul[k] = m_lo
            d_lo = d_lo - e_lo * m_lo
            e_hi = coupling(j + 1)
            m_hi = e_hi * hi
            mul[j + 1] = m_hi
            d_hi = d_hi - e_hi * m_hi
        if j == half:
            e_mid = coupling(half)
            lo = jnp.where(ground <= k, 1.0 / d_lo, 0.0)
            m_mid = e_mid * lo
            mul[half] = m_mid
            d_hi = d_hi - e_mid * m_mid
        else:
            lo = jnp.where(ground <= k, 1.0 / d_lo, 0.0)
        hi = jnp.where(ground <= j, 1.0 / d_hi, 0.0)
        inv[k] = lo
        inv[j] = hi
    one = jnp.ones((ni, nj), F32)
    t0 = [one] + [None] * (half - 1)
    tl = [one] + [None] * (half - 1)
    for s in range(1, half):
        t0[s] = mul[s] * t0[s - 1]
        tl[s] = mul[last - s + 1] * tl[s - 1]
        g0[s] = t0[s]
        gl[last - s] = tl[s]
    g0[0] = one
    gl[last] = one
    xh0 = inv[half] * (mul[half] * t0[half - 1])
    xhl = inv[half] * tl[half - 1]
    xk0 = inv[half - 1] * t0[half - 1] + mul[half] * xh0
    xkl = mul[half] * xhl
    g0[half], gl[half] = xh0, xhl
    g0[half - 1], gl[half - 1] = xk0, xkl
    for s in range(1, half):
        k, j = half - 1 - s, half + s
        xk0 = inv[k] * g0[k] + mul[k + 1] * xk0
        xkl = mul[k + 1] * xkl
        xh0 = mul[j] * xh0
        xhl = inv[j] * gl[j] + mul[j] * xhl
        g0[k], gl[k] = xk0, xkl
        g0[j], gl[j] = xh0, xhl
    planes[0] = g0[0]
    planes[1] = g0[last]
    planes[2] = gl[last]
    planes[3] = c[0]


def condense(group, own, mate, cf):
    lower = group < 2
    is_inner = (group == 1) | (group == 2)
    inner = [jnp.where(is_inner, own[n], mate[n]) for n in range(4)]
    outer = [jnp.where(is_inner, mate[n], own[n]) for n in range(4)]
    x = inner[1]
    g_out, g_in = jnp.where(lower, outer[2], outer[0]), jnp.where(lower, inner[0], inner[2])
    c = jnp.where(lower, inner[3], outer[3])
    kappa = c / (1.0 + c * (g_out + g_in))
    cf[0] = kappa
    cf[1] = jnp.where(lower, inner[2], inner[0]) - kappa * x * x
    cf[2] = jnp.zeros_like(x)
    cf[3] = jnp.zeros_like(x)
    cf[4] = x
    cf[5] = g_out
    cf[6] = g_in
    cf[7] = inner[3]


def spread_setup(groups, group, own, got, st):
    st[group] = own[...]
    for m in range(1, groups):
        st[source_of(group, m, groups)] = got[m - 1][...]


def lane_matrix(nj):
    src = lax.broadcasted_iota(jnp.int32, (2 * nj, nj), 0) % nj
    dst = lax.broadcasted_iota(jnp.int32, (2 * nj, nj), 1)
    return jnp.where(src == dst + 1, 1.0, jnp.where(src == dst - 1, -1.0, 0.0)).astype(jnp.bfloat16)


def lane_difference(x, matrix):
    high = x.astype(jnp.bfloat16)
    low = (x - high.astype(F32)).astype(jnp.bfloat16)
    return jnp.dot(jnp.concatenate([high, low], 1), matrix, preferred_element_type=F32)


def at_lanes(low, high, nj):
    tile = 8
    place = lax.broadcasted_iota(jnp.int32, (tile, nj), 0)
    top = bottom = jnp.zeros((tile, nj), F32)
    for n, row in enumerate(low):
        top = jnp.where(place == n, row, top)
    for n, row in enumerate(high):
        bottom = jnp.where(place == tile - len(high) + n, row, bottom)
    return jnp.concatenate([top, jnp.zeros((nj - 2 * tile, nj), F32), bottom], 0).T


def add_rows(ref, rows):
    for r, plane in rows:
        ref[:, r, :] = ref[:, r, :] + plane


def interior_kernel(first, *refs):
    refs = list(refs)
    take = lambda n: [refs.pop(0) for _ in range(n)]
    zonal, merid, press = take(3)
    uc, vc = (None, None) if first else take(2)
    zonal_out, merid_out, part = take(3)
    pe, ue = take(2)
    depth, ni, nj = press.shape
    per = nj // ni
    rows = per * ni
    matrix = lane_matrix(nj)
    edge = jnp.zeros((depth, nj), F32)
    for ref in (pe, ue):
        ref[:, PAD - 1, :] = edge
        ref[:, PAD + ni, :] = edge
    above, below = slice(PAD + 1, PAD + 1 + ni), slice(PAD - 1, PAD - 1 + ni)
    for b in range(depth // per):
        here = slice(b * per, (b + 1) * per)
        pe[here, PAD : PAD + ni, :] = press[here]
        zonal_out[here] = zonal[here] - H_STEP * (pe[here, above, :] - pe[here, below, :])
    if not first:
        add_rows(zonal_out, ((0, uc[0]), (ni - 1, uc[1])))
    for b in range(depth // per):
        here = slice(b * per, (b + 1) * per)
        p = press[here].reshape(rows, nj)
        ue[here, PAD : PAD + ni, :] = zonal_out[here]
        v = merid[here].reshape(rows, nj)
        if not first:
            v = v + at_lanes((vc[0, b : b + 1, :],), (vc[1, b : b + 1, :],), nj)
        v = v - H_STEP * lane_difference(p, matrix)
        merid_out[here] = v.reshape(per, ni, nj)
        spread = (ue[here, above, :] - ue[here, below, :]).reshape(rows, nj) + lane_difference(v, matrix)
        part[here] = (p - D_STEP * spread).reshape(per, ni, nj)


def emit_kernel(zonal, merid, uc, vc, zonal_out, merid_out):
    depth, ni, nj = zonal.shape
    per = nj // ni
    for b in range(depth // per):
        here = slice(b * per, (b + 1) * per)
        turned = at_lanes((vc[0, b : b + 1, :],), (vc[1, b : b + 1, :],), nj)
        merid_out[here] = merid[here] + turned.reshape(per, ni, nj)
        zonal_out[here] = zonal[here]
    add_rows(zonal_out, ((0, uc[0]), (ni - 1, uc[1])))


def solve_kernel(first, final, hx, hy, groups, *refs):
    refs = list(refs)
    take = lambda n: [refs.pop(0) for _ in range(n)]
    paired = groups == 4
    part0, vert, inv, mul = take(4)
    ox, oy = take(hx.count), take(hy.count)
    rx, ry = take(hx.count), take(hy.count)
    uh, vh = (None, None) if first else take(2)
    if paired:
        own_s, mate_s = take(2) if first else (None, None)
        cf = None if first else take(1)[0]
    y_out, part, planes, uc, vc = take(5)
    across = take(2) if paired else None
    if paired and first:
        cf = take(1)[0]
    uh_out, vh_out = (None, None) if final else take(2)
    rows = take(1)[0]
    depth, ni, nj = part0.shape
    last, half, per = depth - 1, depth // 2, nj // ni
    group = lax.axis_index("lev")
    if paired and first:
        condense(group, own_s, mate_s, cf)

    u_lo = hx.low(rx, 2) if first else uh[0]
    u_hi = hx.high(rx, 2) if first else uh[1]
    u_lo = u_lo - H_STEP * (hx.down(ox, 0) - hx.low(rx, 0))
    u_hi = u_hi - H_STEP * (hx.high(rx, 1) - hx.up(ox, 1))
    u_first, u_last = H_STEP * hx.low(rx, 1), -H_STEP * hx.high(rx, 0)
    uc[0], uc[1] = u_first, u_last
    v_lo = hy.low(ry, 2) if first else vh[0]
    v_hi = hy.high(ry, 2) if first else vh[1]
    v_lo = v_lo - H_STEP * (hy.down(oy, 0) - hy.low(ry, 0))
    v_hi = v_hi - H_STEP * (hy.high(ry, 1) - hy.up(oy, 1))
    if not final:
        uh_out[0], uh_out[1] = u_lo, u_hi
        vh_out[0], vh_out[1] = v_lo, v_hi
    v_first, v_last = H_STEP * hy.low(ry, 1), -H_STEP * hy.high(ry, 0)
    vc[0], vc[1] = v_first, v_last
    edges = ((0, D_STEP * u_lo), (1, D_STEP * u_first), (ni - 2, -D_STEP * u_last), (ni - 1, -D_STEP * u_hi))
    for n, (_, plane) in enumerate(edges):
        rows[n] = plane
    blocks = depth // per
    for b in [x for pair in zip(range(blocks // 2), range(blocks - 1, -1, -1)) for x in pair] + [blocks // 2] * (blocks % 2):
        here, one = slice(b * per, (b + 1) * per), slice(b, b + 1)
        low = (D_STEP * v_lo[one], D_STEP * v_first[one])
        high = (-D_STEP * v_last[one], -D_STEP * v_hi[one])
        part[here] = part0[here] + at_lanes(low, high, nj).reshape(per, ni, nj)
        for n, (r, _) in enumerate(edges):
            part[here, r, :] = part[here, r, :] + rows[n, here]

    lo = vert[0] - V_STEP * part[1]
    hi = vert[last] + V_STEP * part[last - 1]
    y_out[0], y_out[last] = lo, hi
    for s in range(1, half):
        k, j = s, last - s
        lo = (vert[k] - V_STEP * (part[k + 1] - part[k - 1])) + mul[k] * lo
        hi = (vert[j] - V_STEP * (part[j + 1] - part[j - 1])) + mul[j + 1] * hi
        y_out[k], y_out[j] = lo, hi
    hi = inv[half] * (hi + mul[half] * lo)
    lo = inv[half - 1] * lo + mul[half] * hi
    y_out[half], y_out[half - 1] = hi, lo
    for s in range(1, half):
        k, j = half - 1 - s, half + s
        lo = inv[k] * y_out[k] + mul[k + 1] * lo
        hi = inv[j] * y_out[j] + mul[j] * hi
        y_out[k], y_out[j] = lo, hi
    p_first, p_last = part[0], part[last]
    planes[0], planes[1] = lo, hi
    planes[2], planes[3] = p_first, p_last
    if paired:
        lower = group < 2
        sign = jnp.where(lower, V_STEP, -V_STEP)
        y_near, y_far = jnp.where(lower, hi, lo), jnp.where(lower, lo, hi)
        p_near, p_far = jnp.where(lower, p_last, p_first), jnp.where(lower, p_first, p_last)
        gain = cf[4] * cf[0]
        inside = y_near - gain * (cf[5] * (sign * p_far) + y_far)
        outside = cf[4] * (sign * p_near) + gain * (y_near - cf[6] * (sign * p_near))
        inside = jnp.where((group == 1) | (group == 2), inside, outside)
        for message in across:
            message[0], message[1] = inside, p_near
        if first:
            across[0][2], across[0][3] = cf[1], cf[7]


def paired_sources(group, cf, own, mate, crossed, lv):
    lower = group < 2
    is_inner = (group == 1) | (group == 2)
    sign = jnp.where(lower, V_STEP, -V_STEP)
    near = jnp.where(lower, 1, 0)
    slot = jnp.where(is_inner, 0, 1)
    lv[slot] = own[...]
    lv[1 - slot] = mate[...]
    kappa, mine, other, gain, x, g_out, g_in = (cf[n] for n in range(7))
    y_in_near, y_in_far, y_out = lv[0, near], lv[0, 1 - near], lv[1, near]
    p_in_near = sign * lv[0, 2 + near]
    p_in_far = sign * lv[0, 3 - near]
    p_out = sign * lv[1, 2 + near]
    flux = kappa * ((y_out - g_out * p_in_far) - (y_in_far + g_in * p_out))
    here = y_in_near + x * (p_out + flux)
    there = crossed[0][0] + crossed[1][0]
    p_there = sign * jnp.where(is_inner, crossed[1][1], crossed[0][1])
    middle = gain * ((there - here) + (other * p_in_near + mine * p_there))
    n_here = middle - p_there
    n_there = p_in_near - middle
    flux = flux - kappa * x * n_here
    in_far = p_out + flux
    out_near = -(p_in_far + flux)
    near_source = jnp.where(is_inner, n_here, out_near)
    far_source = jnp.where(is_inner, in_far, 0.0)
    alpha = jnp.where(lower, far_source, near_source)
    beta = jnp.where(lower, near_source, far_source)
    under = jnp.where(
        group == 1,
        y_out + g_out * out_near,
        jnp.where(
            group == 2,
            there + other * n_there,
            jnp.where(group == 3, y_in_far + g_in * in_far + x * n_here, 0.0),
        ),
    )
    return alpha, beta, under


def chain_sources(groups, group, st, own, got, lv):
    lv[group] = own[...]
    for m in range(1, groups):
        lv[source_of(group, m, groups)] = got[m - 1][...]
    zero = jnp.zeros(own.shape[1:], F32)
    z_top, z_bot = [], []
    for g in range(groups):
        below = V_STEP * lv[g - 1, 3] if g else zero
        above = V_STEP * lv[g + 1, 2] if g < groups - 1 else zero
        z_top.append(lv[g, 0] + st[g, 0] * below - st[g, 1] * above)
        z_bot.append(lv[g, 1] + st[g, 1] * below - st[g, 2] * above)
    ratios, parts = [zero], [zero]
    for g in range(1, groups):
        cg = st[g, 3]
        down = cg * st[g - 1, 1]
        pivot = 1.0 / (1.0 + cg * (st[g - 1, 2] + st[g, 0]) - down * ratios[-1])
        parts.append((cg * (z_bot[g - 1] - z_top[g]) + down * parts[-1]) * pivot)
        ratios.append(cg * st[g, 1] * pivot)
    flux = [zero] * (groups + 1)
    for g in range(groups - 1, 0, -1):
        flux[g] = parts[g] + ratios[g] * flux[g + 1]
    alpha, beta, under = zero, zero, zero
    for g in range(groups):
        mine = group == g
        if g:
            alpha = jnp.where(mine, V_STEP * lv[g - 1, 3] + flux[g], alpha)
            bot = z_bot[g - 1] + st[g - 1, 1] * flux[g - 1] - st[g - 1, 2] * flux[g]
            under = jnp.where(mine, bot, under)
        if g < groups - 1:
            beta = jnp.where(mine, -(V_STEP * lv[g + 1, 2] + flux[g + 1]), beta)
    return alpha, beta, under


def finish_kernel(groups, first, final, hx, hy, *refs):
    refs = list(refs)
    take = lambda n: [refs.pop(0) for _ in range(n)]
    y, part, g0, gl, own = take(5)
    got = take(groups - 1)
    paired = groups == 4
    system = take(1)[0]
    setups = take(groups) if first and not paired else ()
    vert_out, press_out = take(2)
    mx, my = ([], []) if final else (take(hx.count), take(hy.count))
    if first:
        early, system = system, take(1)[0]
    lv = take(1)[0]
    depth, ni, nj = y.shape
    group = lax.axis_index("lev")
    if paired:
        if first:
            for n in (0, 1, 4, 5, 6):
                system[n] = early[n]
            other = got[1][2]
            c = jnp.where(group < 2, got[1][3], early[7])
            system[2] = other
            system[3] = c / (1.0 + c * (early[1] + other))
        alpha, beta, under = paired_sources(group, system, own, got[0], got[1:], lv)
    else:
        if first:
            spread_setup(groups, group, setups[0], setups[1:], system)
        alpha, beta, under = chain_sources(groups, group, system, own, got, lv)
    vert, press = take(2) if final else (vert_out, press_out)

    def level(k, w_prev):
        w = y[k] + g0[k] * alpha + gl[k] * beta
        vert[k] = w
        press[k] = part[k] - P_STEP * (w - w_prev)
        return w

    if final:
        sems = take(1)[0]
        step, w, copies = max(depth // 4, 1), under, []
        for start in range(0, depth, step):
            stop = min(start + step, depth)
            w = lax.fori_loop(start, stop, level, w, unroll=True)
            for n, (a, b) in enumerate(((vert, vert_out), (press, press_out))):
                here = pl.ds(start, stop - start)
                copies.append(pltpu.make_async_copy(a.at[here], b.at[here], sems.at[n, start // step]))
                copies[-1].start()
        for copy in copies:
            copy.wait()
        return
    both_x, both_y = take(2)
    w, per = under, nj // ni
    for k in range(depth):
        w = level(k, w)
        if (k + 1) % per == 0:
            pack_pressure(press_out, both_x, both_y, k // per)
    hx.write(mx, both_x)
    hy.write(my, both_y)


def body(zonal, meridional, vertical, pressure, coupling, surface, lid_flag):
    depth, ni, nj = coupling.shape
    full, four, two = (depth, ni, nj), (4, ni, nj), (2, ni, nj)
    groups = lax.axis_size("lev")
    hx = Halo("gx", (depth, nj))
    hy = Halo("gy", (depth // (nj // ni), nj))
    wide = pltpu.VMEM((depth, ni + 2 * PAD, nj), F32)

    inputs = (pressure, meridional, zonal)
    results = call(
        functools.partial(first_kernel, hx, hy),
        [full] * 3 + hx.shapes(3) + hy.shapes(3),
        [pltpu.with_memory_space_constraint(a, pltpu.HBM) for a in inputs],
        scratch=[hx.scratch(3), hy.scratch(3), pltpu.SemaphoreType.DMA((3,))],
        spaces=[HBM] * 3,
        types=[a.dtype for a in inputs],
    )
    pressure, meridional, zonal = results[:3]
    ox, oy = results[3 : 3 + hx.count], results[3 + hx.count :]
    ry, rx = hy.exchange(oy), hx.exchange(ox)
    inv, mul, g0, gl, own_s = call(
        functools.partial(factor_kernel, groups), [full] * 4 + [four], [coupling, surface, lid_flag]
    )
    paired = groups == 4
    got_s = [to_lev(own_s, m) for m in range(1, 2 if paired else groups)]
    setup = (8 if paired else 4 * groups, ni, nj)
    system = uh = vh = uc = vc = None
    for substep in range(SUBSTEPS):
        first, final = substep == 0, substep == SUBSTEPS - 1
        args = [zonal, meridional, pressure]
        args += [] if first else [uc, vc]
        zonal, meridional, part = call(
            functools.partial(interior_kernel, first), [full] * 3, args, scratch=[wide, wide]
        )
        args = [part, vertical, inv, mul] + ox + oy + rx + ry
        args += [] if first else [uh, vh]
        if paired:
            args += [own_s] + got_s if first else [system]
        ends = [(2,) + hx.plane, (2,) + hy.plane]
        outs = [full, full, four] + ends
        if paired:
            outs += [four if first else two, two] + ([setup] if first else [])
        outs += [] if final else ends
        results = call(functools.partial(solve_kernel, first, final, hx, hy, groups), outs, args, scratch=[pltpu.VMEM((4,) + hx.plane, F32)])
        y, part, own, uc, vc = results[:5]
        if not final:
            uh, vh = results[-2:]
        if paired:
            got = [to_lev(a, m) for m, a in ((1, own), (2, results[5]), (3, results[6]))]
            if first:
                system = results[7]
        else:
            got = [to_lev(own, m) for m in range(1, groups)]
        if final:
            zonal, meridional = call(emit_kernel, [full] * 2, [zonal, meridional, uc, vc])
        args = [y, part, g0, gl, own] + got + [own_s if system is None else system]
        if first and not paired:
            args += [own_s] + got_s
        outs, scratch = [full, full], [pltpu.VMEM((groups, 4, ni, nj), F32)]
        if not final:
            outs += hx.shapes(2) + hy.shapes(2)
        if first:
            outs += [setup if paired else (groups, 4, ni, nj)]
        if final:
            scratch += [pltpu.VMEM(full, F32)] * 2 + [pltpu.SemaphoreType.DMA((2, 4))]
        else:
            scratch += [hx.scratch(2), hy.scratch(2)]
        results = call(
            functools.partial(finish_kernel, groups, first, final, hx, hy),
            outs,
            args,
            scratch=scratch,
            out_spaces=[HBM] * 2 if final else None,
        )
        vertical, pressure = results[:2]
        if first:
            system = results[-1]
        if not final:
            ox, oy = results[2 : 2 + hx.count], results[2 + hx.count : 2 + hx.count + hy.count]
            ry, rx = hy.exchange(oy), hx.exchange(ox)
    return (zonal, meridional, vertical, pressure)


def solution(mesh):
    block = P("lev", "gx", "gy")
    plane = P("gx", "gy")

    return jax.shard_map(
        body,
        mesh=mesh,
        in_specs=(block,) * 5 + (plane,) * 2,
        out_specs=(block,) * 4,
        check_vma=False,
    )
```
